256 devices in a mesh: gx: 8 (over y, core), gy: 8 (over z), gz: 4 (over x).
Axes of the slice: x: 4, y: 4, z: 8, core: 2. Of those that a mesh axis runs over, the one named last changes fastest.
Arguments:
- rhs: float32 [32, 256, 1024], P('gz', 'gy', 'gx'), may hold values from -6 to 6
- perm_x: float32 [32, 256, 1024], P('gz', 'gy', 'gx'), may hold values from 163.84 to 1638.4
- perm_y: float32 [32, 256, 1024], P('gz', 'gy', 'gx'), may hold values from 0.001 to 0.01
- perm_z: float32 [32, 256, 1024], P('gz', 'gy', 'gx'), may hold values from 0.001 to 0.01
- storage: float32 [32, 256, 1024], P('gz', 'gy', 'gx'), may hold values from 0.002 to 0.02
- perf_cell: int32 [8, 32, 32, 8], P('gx', ('gy', 'gz')), may hold values from 0 to 32767
- perf_well: int32 [8, 32, 32, 8], P('gx', ('gy', 'gz')), may hold values from 0 to 3
- perf_index: float32 [8, 32, 32, 8], P('gx', ('gy', 'gz')), may hold values from 0.64 to 6.4
- seg_count: int32 [8, 32, 4], P('gx', ('gy', 'gz')), may hold values from 1 to 4
- bhp: float32 [8, 32, 4], P('gx', ('gy', 'gz')), may hold values from -6 to 6
Outputs:
- pressure: float32 [32, 256, 1024], P('gz', 'gy', 'gx')
- well_residual: float32 [8, 32, 4], P('gx', ('gy', 'gz'))
The draws below stay inside these ranges and needn't reach their ends.
All inputs are finite; a program needn't handle non-finite values.
Results may differ from the reference program's by a relative error of at most 0.002.
Values sent between devices are 32-bit elements; how exact they have to be, the bound alone decides.
A program may use at most 64 MiB of HBM per device.

```python
import math
import jax
import jax.numpy as jnp
from jax import lax

CX = 128
CY = 32
CZ = 8
WO = 4
CAP = 8
SEG = 4
NG = 32
NX = 1024
NY = 256
NZ = 32
CELLS = 32768
N_GX = 8
N_GZ = 4


def plant(entries, stream_key, least, high):
    longest = entries.shape.index(max(entries.shape))
    spots = []
    for shift in (0, 1):
        where = [jax.random.randint(jax.random.fold_in(stream_key, axis), (), 0, length) for axis, length in enumerate(entries.shape)]
        where[longest] = (where[longest] + shift) % entries.shape[longest]
        spots.append(tuple(where))
    return entries.at[spots[0]].set(least).at[spots[1]].set(high)


def levels(key, extent, split, least, top_value):
    factor_of = 1.0
    for dim, shards_of in split:
        draws = jax.random.uniform(jax.random.fold_in(jax.random.fold_in(key, 6), dim), (shards_of,), jnp.float32, least / len(split), top_value / len(split))
        factor_of = factor_of * jnp.repeat(jnp.exp(draws), extent[dim] // shards_of).reshape((-1,) + (1,) * (len(extent) - 1 - dim))
    return factor_of


def normal_values(own_key, shape, width, limit, pieces=(), kind=jnp.bfloat16):
    entries = jax.random.normal(own_key, shape, jnp.float32) * width
    if len(pieces) > 0:
        entries = levels(own_key, shape, pieces, -0.22, 0.18) * entries
    return jnp.clip(entries, min=-limit, max=limit).astype(kind)


def setup_inputs(seed: int = 0) -> dict:
    streams_of = jax.random.split(jax.random.key(seed), 11)
    return {
        "rhs": normal_values(streams_of[0], (NZ, NY, NX), 1.0, 6.0, ((0, 4), (1, 8), (2, 8)), jnp.float32),
        "perm_x": jnp.clip(jnp.exp(math.log(1638.4) - 2.3025851 * jax.random.uniform(streams_of[1], (NZ, NY, NX), jnp.float32) ** levels(streams_of[1], (NZ, NY, NX), ((0, 4), (1, 8), (2, 8)), -0.2, 0.2)), 163.84, 1638.4),
        "perm_y": jnp.clip(jnp.exp(math.log(0.01) - 2.30258502 * jax.random.uniform(streams_of[2], (NZ, NY, NX), jnp.float32) ** levels(streams_of[2], (NZ, NY, NX), ((0, 4), (1, 8), (2, 8)), -0.2, 0.2)), 0.001, 0.01),
        "perm_z": jnp.clip(jnp.exp(math.log(0.01) - 2.30258502 * jax.random.uniform(streams_of[3], (NZ, NY, NX), jnp.float32) ** levels(streams_of[3], (NZ, NY, NX), ((0, 4), (1, 8), (2, 8)), -0.2, 0.2)), 0.001, 0.01),
        "storage": jnp.clip(jnp.exp(math.log(0.02) - 2.30258502 * jax.random.uniform(streams_of[4], (NZ, NY, NX), jnp.float32) ** levels(streams_of[4], (NZ, NY, NX), ((0, 4), (1, 8), (2, 8)), -0.2, 0.2)), 0.002, 0.02),
        "perf_cell": plant(jax.random.randint(streams_of[5], (N_GX, NG, NG, CAP), 0, CELLS), jax.random.fold_in(streams_of[5], 1), 0, CELLS - 1).astype(jnp.int32),
        "perf_well": plant(jax.random.randint(streams_of[6], (N_GX, NG, NG, CAP), 0, WO), jax.random.fold_in(streams_of[6], 1), 0, WO - 1).astype(jnp.int32),
        "perf_index": jnp.clip(jnp.exp(math.log(6.4) - 2.3025851 * jax.random.uniform(streams_of[7], (N_GX, NG, NG, CAP), jnp.float32) ** levels(streams_of[7], (N_GX, NG, NG, CAP), ((0, 8), (1, 32)), -0.2, 0.2)), 0.64, 6.4),
        "seg_count": plant(jax.random.randint(streams_of[8], (N_GX, NG, WO), 1, SEG + 1), jax.random.fold_in(streams_of[8], 1), 1, SEG).astype(jnp.int32),
        "bhp": normal_values(streams_of[9], (N_GX, NG, WO), 1.0, 6.0, ((0, 8), (1, 32)), jnp.float32),
    }


bore_conductance = 20.0


def harmonic(lower_side, upper_side):
    return 2.0 * lower_side * upper_side / (lower_side + upper_side)


def face_values(permeability, axis_number):
    widths = [(0, 0), (0, 0), (0, 0)]
    widths[axis_number] = (1, 1)
    padded = jnp.pad(permeability, widths)
    count_all = padded.shape[axis_number]
    lower_side = lax.slice_in_dim(padded, 0, count_all - 1, axis=axis_number)
    upper_side = lax.slice_in_dim(padded, 1, count_all, axis=axis_number)
    return harmonic(lower_side, upper_side)


def thomas(lower_band, center, upper_band, sources):
    def forward(state_pair, step_items):
        prev_upper, prev_value = state_pair
        low_coef, mid_coef, high_coef, source_now = step_items
        pivot_value = mid_coef - low_coef * prev_upper
        next_upper = high_coef / pivot_value
        next_value = (source_now - low_coef * prev_value) / pivot_value
        return (next_upper, next_value), (next_upper, next_value)

    initial = (jnp.zeros_like(center[0]), jnp.zeros_like(center[0]))
    final_state, stacked = lax.scan(forward, initial, (lower_band, center, upper_band, sources))
    uppers, reduced_values = stacked

    def backward(later_value, step_items):
        upper_now, value_now = step_items
        solved_now = value_now - upper_now * later_value
        return solved_now, solved_now

    last_state, solved = lax.scan(backward, jnp.zeros_like(center[0]), (uppers, reduced_values), reverse=True)
    return solved


def reference(rhs, perm_x, perm_y, perm_z, storage, perf_cell, perf_well, perf_index, seg_count, bhp):
    faces_x = face_values(perm_x, 2)
    faces_y = face_values(perm_y, 1)
    faces_z = face_values(perm_z, 0)
    x_lower = faces_x[:, :, :-1]
    x_upper = faces_x[:, :, 1:]
    y_lower = faces_y[:, :-1, :]
    y_upper = faces_y[:, 1:, :]
    z_lower = faces_z[:-1]
    z_upper = faces_z[1:]
    center = storage + x_lower + x_upper + y_lower + y_upper + z_lower + z_upper

    def apply_full(pressure_field):
        padded = jnp.pad(pressure_field, 1)
        beside = x_lower * padded[1:-1, 1:-1, :-2] + x_upper * padded[1:-1, 1:-1, 2:]
        beside = beside + y_lower * padded[1:-1, :-2, 1:-1] + y_upper * padded[1:-1, 2:, 1:-1]
        beside = beside + z_lower * padded[:-2, 1:-1, 1:-1] + z_upper * padded[2:, 1:-1, 1:-1]
        return center * pressure_field - beside

    def to_lines(pressure_field):
        return pressure_field.reshape(-1, NX).T

    lower_lines = to_lines(-x_lower)
    upper_lines = to_lines(-x_upper)
    center_lines = to_lines(center)

    def line_solve(sources):
        solved = thomas(lower_lines, center_lines, upper_lines, to_lines(sources))
        return solved.T.reshape(NZ, NY, NX)

    column = jnp.arange(N_GX).astype(jnp.int32).reshape(-1, 1, 1, 1)
    source_pos = jnp.arange(NG).astype(jnp.int32).reshape(1, -1, 1, 1)
    owner_pos = jnp.arange(NG).astype(jnp.int32).reshape(1, 1, -1, 1)
    layer = (source_pos % N_GZ) * CZ + perf_cell // (CY * CX)
    row_y = (source_pos // N_GZ) * CY + (perf_cell // CX) % CY
    row_x = column * CX + perf_cell % CX
    count_well = seg_count[column, owner_pos, perf_well]
    segment = (source_pos % N_GZ) * count_well // N_GZ
    segment_id = ((column * NG + owner_pos) * WO + perf_well) * SEG + segment
    total_slots = N_GX * NG * WO * SEG
    flat_id = segment_id.reshape(-1)
    flat_layer = layer.reshape(-1)
    flat_row_y = row_y.reshape(-1)
    flat_row_x = row_x.reshape(-1)
    weights = perf_index.reshape(-1)
    seg_weight = jax.ops.segment_sum(weights, flat_id, num_segments=total_slots)
    bore_pressure = jnp.repeat(bhp.reshape(-1), SEG)

    def segment_pressure(pressure_field):
        perforated = pressure_field[flat_layer, flat_row_y, flat_row_x]
        inflow = jax.ops.segment_sum(weights * perforated, flat_id, num_segments=total_slots)
        return (inflow + bore_conductance * bore_pressure) / (seg_weight + bore_conductance), perforated

    def well_term(pressure_field):
        pressures, perforated = segment_pressure(pressure_field)
        flow_terms = weights * (perforated - pressures[flat_id])
        return jnp.zeros_like(pressure_field).at[flat_layer, flat_row_y, flat_row_x].add(flow_terms)

    first_pass = line_solve(rhs - well_term(jnp.zeros_like(rhs)))
    pressure = first_pass + line_solve(rhs - apply_full(first_pass) - well_term(first_pass))
    final_segments, final_perforated = segment_pressure(pressure)
    well_residual = jnp.sum((final_segments - bore_pressure).reshape(N_GX, NG, WO, SEG), axis=-1)
    return pressure, well_residual
```

```python
import functools

import jax
import jax.numpy as jnp
from jax import lax
from jax.experimental import pallas as pl
from jax.experimental.pallas import tpu as pltpu
from jax.sharding import PartitionSpec as P

F32 = jnp.float32
BF16 = jnp.bfloat16
MESH = pl.DeviceIdType.MESH
LANES = 128
SEG = 4
BORE = 20.0


def harmonic(a, b):
    return 2.0 * a * b / (a + b)


def lane_of(shape):
    return lax.broadcasted_iota(jnp.int32, shape, len(shape) - 1)


def row_of(shape):
    return lax.broadcasted_iota(jnp.int32, shape, len(shape) - 2)


def split_lanes(x):
    high = x.astype(BF16)
    low = (x - high.astype(F32)).astype(BF16)
    return jnp.concatenate([high, low], axis=1)


def onehot_product(selector, x):
    both = jnp.dot(selector, split_lanes(x), preferred_element_type=F32)
    return both[:, :LANES] + both[:, LANES:]


def lane_spread(x, lane, shape):
    return jnp.broadcast_to(x[:, lane : lane + 1], shape)


def pack_ends(pieces):
    pair = lane_of((8, LANES)) // 2
    packed = jnp.zeros((8, LANES), F32)
    for j, piece in enumerate(pieces):
        packed = jnp.where(pair == j, pltpu.roll(piece, 2 * j + 1, 1), packed)
    return packed


def kernel(
    dims, cell_ref, well_ref, wgt_ref, cnt_ref, bhp_ref, rhs_in, px_in, py_in, pz_in, st_in, p_out, res_out,
    rhs, px, py, pz, st, sig, left, right, ylo, yup, zface, alpha, gamma, inv, low_w, high_w, src, field,
    hot_x, hot_dw, line_sel, line_sel_t,
    yperm, zperm, yp, ysend_perm, ysend_p, zp,
    sw_send, sw_all, row_send, rows_a, rows_b, stat_all, ports_a, ports_b, port_send,
    coef_seg, coef_mine,
    in_sem, out_sem, halo_send, halo_recv, fan_send, fan_recv,
):
    nx, ny, nz, zc, yc, wells = dims
    ng = ny * nz
    lines = zc * yc
    pieces = lines // 8
    mx, my, mz = lax.axis_index("gx"), lax.axis_index("gy"), lax.axis_index("gz")
    mg = my * nz + mz

    loads = [
        pltpu.make_async_copy(a, b, in_sem.at[i])
        for i, (a, b) in enumerate(((py_in, py), (pz_in, pz), (px_in, px), (st_in, st), (rhs_in, rhs)))
    ]
    for load in loads:
        load.start()

    barrier = pltpu.get_barrier_semaphore()

    def greet_x(t, c):
        pl.semaphore_signal(barrier, inc=1, device_id={"gx": lax.rem(mx + t, nx)}, device_id_type=MESH)
        return c

    def greet_group(t, c):
        peer = lax.rem(mg + t, ng)
        pl.semaphore_signal(
            barrier, inc=1, device_id={"gy": lax.div(peer, nz), "gz": lax.rem(peer, nz)}, device_id_type=MESH
        )
        return c

    lax.fori_loop(1, ng, greet_group, 0)
    lax.fori_loop(1, nx, greet_x, 0)

    code = cell_ref[...]
    wellv = well_ref[...]
    wgtv = wgt_ref[...]
    lane8 = lane_of((8, LANES))
    sw_row = jnp.zeros((8, LANES), F32)
    for d in range(ng):
        rows = slice(d * 8, d * 8 + 8)
        c = lane_spread(code, d, (8, LANES))
        w = lane_spread(wgtv, d, (8, LANES))
        x = jnp.bitwise_and(c, LANES - 1)
        hot_x[rows, :] = jnp.where(lane8 == x, 1.0, 0.0)
        mine = jnp.where(lane8 == lane_spread(wellv, d, (8, LANES)) + d * wells, 1.0, 0.0)
        mine = mine * w
        hot_dw[rows, :] = mine
        sw_row = sw_row + mine
    sw_send[0] = jnp.sum(sw_row, axis=0, keepdims=True)
    lane1 = lane_of((1, LANES))
    counts = jnp.zeros((1, LANES), F32)
    bores = jnp.zeros((1, LANES), F32)
    for w in range(wells):
        here = lane1 == mg * wells + w
        counts = jnp.where(here, cnt_ref[0, w].astype(F32), counts)
        bores = jnp.where(here, bhp_ref[0, w], bores)
    sw_send[1] = counts
    sw_send[2] = bores

    def fan_group(source, target, which):
        def step(t, c):
            peer = lax.rem(mg + t, ng)
            pltpu.make_async_remote_copy(
                src_ref=source, dst_ref=target.at[mg], send_sem=fan_send.at[which], recv_sem=fan_recv.at[which],
                device_id={"gy": lax.div(peer, nz), "gz": lax.rem(peer, nz)}, device_id_type=MESH,
            ).start()
            return c

        lax.fori_loop(1, ng, step, 0)

    def fan_x(source, target, which):
        def step(t, c):
            pltpu.make_async_remote_copy(
                src_ref=source, dst_ref=target.at[mx], send_sem=fan_send.at[which], recv_sem=fan_recv.at[which],
                device_id={"gx": lax.rem(mx + t, nx)}, device_id_type=MESH,
            ).start()
            return c

        lax.fori_loop(1, nx, step, 0)

    def fan_wait(target, count, sems, which):
        view = target.at[pl.ds(0, count)]
        pltpu.make_async_copy(view, view, sems.at[which]).wait()

    y_next, y_prev = lax.rem(my + 1, ny), lax.rem(my + ny - 1, ny)
    z_next, z_prev = lax.rem(mz + 1, nz), lax.rem(mz + nz - 1, nz)

    def halo_copy(source, target, which, peer):
        return pltpu.make_async_remote_copy(
            src_ref=source, dst_ref=target, send_sem=halo_send.at[which], recv_sem=halo_recv.at[which],
            device_id=peer, device_id_type=MESH,
        )

    def halos(y_src, y_dst, z_src, z_dst, base):
        last = pl.ds((zc - 1) * yc, yc)
        return [
            halo_copy(y_src.at[0], y_dst.at[1], base, {"gy": y_prev}),
            halo_copy(y_src.at[1], y_dst.at[0], base + 1, {"gy": y_next}),
            halo_copy(z_src.at[pl.ds(0, yc)], z_dst.at[1], base + 2, {"gz": z_prev}),
            halo_copy(z_src.at[last], z_dst.at[0], base + 3, {"gz": z_next}),
        ]

    loads[0].wait()
    loads[1].wait()
    for z in range(zc):
        ysend_perm[0, z] = py[z * yc : z * yc + 1, :]
        ysend_perm[1, z] = py[z * yc + yc - 1 : z * yc + yc, :]

    pl.semaphore_wait(barrier, ng - 1 + nx - 1)
    fan_group(sw_send, sw_all, 0)
    perm_halos = halos(ysend_perm, yperm, pz, zperm, 0)
    for copy in perm_halos:
        copy.start()
    sw_all[mg] = sw_send[...]

    for half in range(lines // LANES):
        for d in range(ng):
            line = jnp.right_shift(lane_spread(code, d, (8, LANES)), 7) - half * LANES
            line_sel[d * 8 : d * 8 + 8, half * LANES : half * LANES + LANES] = jnp.where(lane8 == line, 1.0, 0.0)
    line_sel_t[...] = line_sel[...].T.astype(BF16)

    loads[2].wait()
    loads[3].wait()
    lane_s = lane_of((yc, LANES))
    row_s = row_of((yc, LANES))
    for z in range(zc):
        rows = slice(z * yc, z * yc + yc)
        v = px[rows, :]
        f = jnp.where(lane_s == 0, 0.0, harmonic(pltpu.roll(v, 1, 1), v))
        left[rows, :] = f
        right[rows, :] = pltpu.roll(f, LANES - 1, 1)
    for copy in perm_halos:
        copy.wait_recv()
    for z in range(zc):
        rows = slice(z * yc, z * yc + yc)
        v = py[rows, :]
        below = jnp.where(row_s == 0, yperm[0, z], pltpu.roll(v, 1, 0))
        f = harmonic(below, v)
        f = jnp.where(jnp.logical_and(row_s == 0, my == 0), 0.0, f)
        top = harmonic(py[z * yc + yc - 1 : z * yc + yc, :], yperm[1, z])
        top = jnp.where(my == ny - 1, 0.0, top)
        g = jnp.where(row_s == yc - 1, top, pltpu.roll(f, yc - 1, 0))
        ylo[rows, :] = f
        yup[rows, :] = g
        sig[rows, :] = st[rows, :] + f + g
    before = zperm[0]
    for z in range(zc + 1):
        v = pz[z * yc : z * yc + yc, :] if z < zc else zperm[1]
        f = harmonic(before, v)
        if z == 0:
            f = jnp.where(mz == 0, 0.0, f)
        if z == zc:
            f = jnp.where(mz == nz - 1, 0.0, f)
        zface[z * yc : z * yc + yc, :] = f
        before = v
    for z in range(zc):
        rows = slice(z * yc, z * yc + yc)
        sig[rows, :] = sig[rows, :] + zface[rows, :] + zface[z * yc + yc : z * yc + 2 * yc, :]

    chunk = 64
    lane_c = lane_of((chunk, LANES))
    strides = [1 << i for i in range(7)]

    def reduce_matrix(i, carry):
        rows = pl.ds(pl.multiple_of(i * chunk, chunk), chunk)
        lo, hi, s = left[rows, :], right[rows, :], sig[rows, :]
        for level, stride in enumerate(strides):
            r = 1.0 / (s + lo + hi)
            from_low = lane_c > stride
            from_high = lane_c < LANES - 1 - stride
            a = jnp.where(from_low, lo * pltpu.roll(r, stride, 1), 0.0)
            g = jnp.where(from_high, hi * pltpu.roll(r, LANES - stride, 1), 0.0)
            s = s + a * pltpu.roll(s, stride, 1) + g * pltpu.roll(s, LANES - stride, 1)
            lo = jnp.where(from_low, a * pltpu.roll(lo, stride, 1), lo)
            hi = jnp.where(from_high, g * pltpu.roll(hi, LANES - stride, 1), hi)
            alpha[level, rows, :] = a
            gamma[level, rows, :] = g
        r = 1.0 / (s + lo + hi)
        first, last = lane_c == 0, lane_c == LANES - 1
        end = jnp.logical_or(first, last)
        inv[rows, :] = jnp.where(end, 0.0, r)
        low_w[rows, :] = jnp.where(first, 1.0, jnp.where(last, 0.0, lo * r))
        high_w[rows, :] = jnp.where(last, 1.0, jnp.where(first, 0.0, hi * r))
        sig[rows, :] = s
        right[rows, :] = hi
        return carry

    lax.fori_loop(0, lines // chunk, reduce_matrix, 0)

    def ends_of(ref):
        return pack_ends([ref[j * 8 : j * 8 + 8, :] for j in range(pieces)])

    stat_all[mx, 0] = ends_of(sig) + pltpu.roll(ends_of(px), LANES // 2, 1)
    stat_all[mx, 1] = ends_of(right)
    fan_x(stat_all.at[mx], stat_all, 1)

    fan_wait(sw_all, ng - 1, fan_recv, 0)
    total = jnp.zeros((3, 1, LANES), F32)
    for s in range(ng):
        total = total + sw_all[s]
    count, bore = total[1], total[2]

    def slot_of(g):
        return jnp.floor(g * count * (1.0 / nz))

    layer_slots = [slot_of(float(g)) for g in range(nz)]
    layer_sw = [sum(sw_all[y * nz + g, 0] for y in range(ny)) for g in range(nz)]
    layer_inv = []
    layer_seg = []
    for g in range(nz):
        same = sum(jnp.where(layer_slots[h] == layer_slots[g], layer_sw[h], 0.0) for h in range(nz))
        layer_seg.append(same)
        layer_inv.append(1.0 / (same + BORE))
    my_slot = slot_of(mz.astype(F32))
    my_inv = jnp.zeros((1, LANES), F32)
    for g in range(nz):
        my_inv = jnp.where(mz == g, layer_inv[g], my_inv)
    for g in range(nz):
        coef_seg[g] = layer_inv[g]
        coef_mine[g] = jnp.where(layer_slots[g] == my_slot, 1.0, 0.0) * my_inv
    my_base = BORE * bore * my_inv

    def well_sources(pressure_cols, seg_row):
        drop = seg_row if pressure_cols is None else seg_row - pressure_cols
        back = jnp.sum(hot_dw[...] * drop, axis=1, keepdims=True)
        return onehot_product(line_sel_t[...], hot_x[...] * back)

    def solve_local(b_ref):
        half = lines // 2
        ends = []
        for h in range(2):
            rows = slice(h * half, h * half + half)
            b = b_ref[rows, :]
            for level, stride in enumerate(strides):
                b = b + alpha[level, rows, :] * pltpu.roll(b, stride, 1) + gamma[level, rows, :] * pltpu.roll(
                    b, LANES - stride, 1
                )
            b_ref[rows, :] = b
            ends += [b[j * 8 : j * 8 + 8, :] for j in range(half // 8)]
        packed = pack_ends(ends)
        return packed + pltpu.roll(packed, LANES // 2, 1)

    loads[4].wait()
    src[...] = rhs[...] + well_sources(None, my_base)
    ports_a[mx] = solve_local(src)
    fan_x(ports_a.at[mx], ports_a, 2)

    fan_wait(stat_all, nx - 1, fan_recv, 1)

    def ends_at(k):
        s, c = stat_all[k, 0], stat_all[k, 1]
        return dict(
            sz=s, sf=pltpu.roll(s, LANES - 1, 1), pz=pltpu.roll(s, LANES // 2, 1),
            pf=pltpu.roll(s, LANES // 2 - 1, 1), c=pltpu.roll(c, LANES - 1, 1),
        )

    own = ends_at(mx)

    def walk(direction):
        chain = []
        for t in range(1, nx):
            k = mx + direction * t
            valid = jnp.logical_and(k >= 0, k < nx)
            chain.append((jnp.clip(k, 0, nx - 1), valid))
        blocks = [ends_at(k) for k, _ in chain]
        ground = jnp.zeros((8, LANES), F32)
        factors = [None] * (nx - 1)
        for t in range(nx - 1, 0, -1):
            b = blocks[t - 1]
            nearer = own if t == 1 else blocks[t - 2]
            far, near, edge = ("sf", "sz", ("pz", "pf")) if direction < 0 else ("sz", "sf", ("pf", "pz"))
            face = jnp.where(chain[t - 1][1], harmonic(b[edge[0]], nearer[edge[1]]), 0.0)
            through = b["c"] / (b["c"] + b[far] + ground)
            inner = b[near] + (b[far] + ground) * through
            outward = face / (face + inner)
            ground = inner * outward
            factors[t - 1] = (through, outward)
        reach = jnp.ones((8, LANES), F32)
        weights = []
        for through, outward in factors:
            near_w = reach * outward
            reach = near_w * through
            weights.append((near_w, reach))
        return ground, weights, [k for k, _ in chain]

    ground_l, weights_l, index_l = walk(-1)
    ground_r, weights_r, index_r = walk(1)
    a, e, c = own["sf"] + ground_l, own["sz"] + ground_r, own["c"]
    scale = 1.0 / (a * e + (a + e) * c)
    ff, fz, zz = (e + c) * scale, c * scale, (a + c) * scale
    even = lane8 % 2 == 0
    lower_half = lane8 < LANES // 2

    def weave(z_first, f_first, z_last, f_last):
        first = jnp.where(even, z_first, pltpu.roll(f_first, 1, 1))
        last = jnp.where(even, pltpu.roll(z_last, LANES // 2, 1), pltpu.roll(f_last, LANES // 2 + 1, 1))
        return jnp.where(lower_half, first, last)

    terms = [(mx, weave(fz, ff, zz, fz))]
    for (near_w, far_w), k in zip(weights_l, index_l):
        terms.append((k, weave(ff * near_w, ff * far_w, fz * near_w, fz * far_w)))
    for (near_w, far_w), k in zip(weights_r, index_r):
        terms.append((k, weave(fz * far_w, fz * near_w, zz * far_w, zz * near_w)))

    def join(ports, b_ref, write):
        ends = sum(w * ports[k] for k, w in terms)
        ends = ends + pltpu.roll(ends, LANES - 1, 1)
        for j in range(pieces):
            rows = slice(j * 8, j * 8 + 8)
            first = lane_spread(ends, 2 * j, (8, LANES))
            last = lane_spread(ends, LANES // 2 + 2 * j, (8, LANES))
            write(rows, b_ref[rows, :] * inv[rows, :] + low_w[rows, :] * first + high_w[rows, :] * last)

    def perforated():
        rows = onehot_product(line_sel[...].astype(BF16), field[...])
        cols = jnp.sum(rows * hot_x[...], axis=1, keepdims=True)
        return cols, jnp.sum(hot_dw[...] * cols, axis=0, keepdims=True)

    fan_wait(ports_a, nx - 1, fan_recv, 2)

    def write_first(rows, value):
        field[rows, :] = value

    join(ports_a, src, write_first)
    for z in range(zc):
        ysend_p[0, z] = field[z * yc : z * yc + 1, :]
        ysend_p[1, z] = field[z * yc + yc - 1 : z * yc + yc, :]
    p_halos = halos(ysend_p, yp, field, zp, 4)
    for copy in p_halos:
        copy.start()
    cols, row = perforated()
    row_send[0] = row
    fan_group(row_send.at[0], rows_a, 3)
    rows_a[mg] = row

    for copy in p_halos:
        copy.wait_recv()
    for z in range(zc):
        rows = slice(z * yc, z * yc + yc)
        v = field[rows, :]
        below = jnp.where(row_s == 0, yp[0, z], pltpu.roll(v, 1, 0))
        above = jnp.where(row_s == yc - 1, yp[1, z], pltpu.roll(v, yc - 1, 0))
        under = field[z * yc - yc : z * yc, :] if z > 0 else zp[0]
        over = field[z * yc + yc : z * yc + 2 * yc, :] if z < zc - 1 else zp[1]
        beside = ylo[rows, :] * below + yup[rows, :] * above
        beside = beside + zface[rows, :] * under + zface[z * yc + yc : z * yc + 2 * yc, :] * over
        src[rows, :] = rhs[rows, :] + beside

    fan_wait(rows_a, ng - 1, fan_recv, 3)
    seg_row = my_base
    for g in range(nz):
        seg_row = seg_row + coef_mine[g] * sum(rows_a[y * nz + g] for y in range(ny))
    src[...] = src[...] + well_sources(cols, seg_row)

    ports_b[mx] = solve_local(src)
    fan_x(ports_b.at[mx], ports_b, 4)
    for copy in p_halos:
        copy.wait_send()
    fan_wait(ports_b, nx - 1, fan_recv, 4)

    join(ports_b, src, write_first)
    store = pltpu.make_async_copy(field, p_out, out_sem)
    store.start()
    _, row = perforated()
    row_send[1] = row
    fan_group(row_send.at[1], rows_b, 5)
    rows_b[mg] = row
    fan_wait(rows_b, ng - 1, fan_recv, 5)
    res = jnp.zeros((1, LANES), F32)
    for g in range(nz):
        inflow = sum(rows_b[y * nz + g] - bore * sw_all[y * nz + g, 0] for y in range(ny))
        res = res + coef_seg[g] * inflow
    res_out[...] = res

    store.wait()
    for copy in perm_halos:
        copy.wait_send()
    fan_wait(sw_all, ng - 1, fan_send, 0)
    fan_wait(stat_all, nx - 1, fan_send, 1)
    fan_wait(ports_a, nx - 1, fan_send, 2)
    fan_wait(rows_a, ng - 1, fan_send, 3)
    fan_wait(ports_b, nx - 1, fan_send, 4)
    fan_wait(rows_b, ng - 1, fan_send, 5)


def shards(dims, rhs, perm_x, perm_y, perm_z, storage, perf_cell, perf_well, perf_index, seg_count, bhp):
    nx, ny, nz, zc, yc, wells = dims
    ng = ny * nz
    lines = zc * yc
    perfs = ng * 8
    plane = (lines, LANES)
    flat = [a.reshape(plane) for a in (rhs, perm_x, perm_y, perm_z, storage)]
    slots = [a[0, 0].T for a in (perf_cell, perf_well, perf_index)]
    vmem = pl.BlockSpec(memory_space=pltpu.VMEM)
    smem = pl.BlockSpec(memory_space=pltpu.SMEM)
    anywhere = pl.BlockSpec(memory_space=pl.ANY)
    whole = pltpu.VMEM(plane, F32)
    perf_plane = pltpu.VMEM((perfs, LANES), F32)
    pressure, residual = pl.pallas_call(
        functools.partial(kernel, dims),
        out_shape=(jax.ShapeDtypeStruct(plane, F32), jax.ShapeDtypeStruct((1, LANES), F32)),
        in_specs=[vmem] * 3 + [smem] * 2 + [anywhere] * 5,
        out_specs=(anywhere, vmem),
        scratch_shapes=[whole] * 5
        + [whole] * 5
        + [pltpu.VMEM((lines + yc, LANES), F32)]
        + [pltpu.VMEM((7, lines, LANES), F32)] * 2
        + [whole] * 5
        + [perf_plane] * 2
        + [pltpu.VMEM((perfs, lines), F32), pltpu.VMEM((lines, perfs), BF16)]
        + [pltpu.VMEM((2, zc, 1, LANES), F32), pltpu.VMEM((2, yc, LANES), F32)]
        + [pltpu.VMEM((2, zc, 1, LANES), F32)] * 3
        + [pltpu.VMEM((2, yc, LANES), F32)]
        + [pltpu.VMEM((3, 1, LANES), F32), pltpu.VMEM((ng, 3, 1, LANES), F32)]
        + [pltpu.VMEM((2, 1, LANES), F32)]
        + [pltpu.VMEM((ng, 1, LANES), F32)] * 2
        + [pltpu.VMEM((nx, 2, 8, LANES), F32)]
        + [pltpu.VMEM((nx, 8, LANES), F32)] * 2
        + [pltpu.VMEM((8, LANES), F32)]
        + [pltpu.VMEM((nz, 1, LANES), F32)] * 2
        + [
            pltpu.SemaphoreType.DMA((5,)),
            pltpu.SemaphoreType.DMA,
            pltpu.SemaphoreType.DMA((8,)),
            pltpu.SemaphoreType.DMA((8,)),
            pltpu.SemaphoreType.DMA((6,)),
            pltpu.SemaphoreType.DMA((6,)),
        ],
        compiler_params=pltpu.CompilerParams(
            collective_id=0, has_side_effects=True, vmem_limit_bytes=32 * 1024 * 1024
        ),
        name="sweeps",
    )(*slots, seg_count[0], bhp[0], *flat)
    position = lax.axis_index("gy") * nz + lax.axis_index("gz")
    mine = lax.dynamic_slice(residual, (0, position * wells), (1, wells))
    return pressure.reshape(rhs.shape), mine.reshape(1, 1, wells)


def solution(mesh):
    nx, ny, nz = mesh.shape["gx"], mesh.shape["gy"], mesh.shape["gz"]
    cells = P("gz", "gy", "gx")
    perfs = P("gx", ("gy", "gz"), None, None)
    owned = P("gx", ("gy", "gz"), None)

    def program(rhs, perm_x, perm_y, perm_z, storage, perf_cell, perf_well, perf_index, seg_count, bhp):
        dims = (nx, ny, nz, rhs.shape[0] // nz, rhs.shape[1] // ny, seg_count.shape[-1])
        return jax.shard_map(
            functools.partial(shards, dims),
            mesh=mesh,
            in_specs=(cells,) * 5 + (perfs,) * 3 + (owned,) * 2,
            out_specs=(cells, owned),
            check_vma=False,
        )(rhs, perm_x, perm_y, perm_z, storage, perf_cell, perf_well, perf_index, seg_count, bhp)

    return program
```

```python
import functools

import jax
import jax.numpy as jnp
from jax import lax
from jax.experimental import pallas as pl
from jax.experimental.pallas import tpu as pltpu
from jax.sharding import PartitionSpec as P

F32 = jnp.float32
BF16 = jnp.bfloat16
MESH = pl.DeviceIdType.MESH
LANES = 128
SEG = 4
BORE = 20.0


def harmonic(a, b):
    return 2.0 * a * b / (a + b)


def lane_of(shape):
    return lax.broadcasted_iota(jnp.int32, shape, len(shape) - 1)


def row_of(shape):
    return lax.broadcasted_iota(jnp.int32, shape, len(shape) - 2)


def split_lanes(x):
    high = x.astype(BF16)
    low = (x - high.astype(F32)).astype(BF16)
    return jnp.concatenate([high, low], axis=1)


def onehot_product(selector, x):
    both = jnp.dot(selector, split_lanes(x), preferred_element_type=F32)
    return both[:, :LANES] + both[:, LANES:]


def lane_spread(x, lane, shape):
    return jnp.broadcast_to(x[:, lane : lane + 1], shape)


def pack_ends(pieces):
    pair = lane_of((8, LANES)) // 2
    packed = jnp.zeros((8, LANES), F32)
    for j, piece in enumerate(pieces):
        packed = jnp.where(pair == j, pltpu.roll(piece, 2 * j + 1, 1), packed)
    return packed


def kernel(
    dims, cell_in, well_in, wgt_in, cnt_in, bhp_in, rhs_in, px_in, py_in, pz_in, st_in, p_out, res_out,
    cell_ref, well_ref, wgt_ref, cnt_ref, bhp_ref, rhs, px, py, pz, st, sig, left, right, ylo, yup, zface, alpha, gamma, inv, low_w, high_w, src, field,
    hot_x, hot_dw, line_sel, line_sel_t,
    yperm, zperm, yp, ysend_perm, ysend_p, zp,
    sw_send, sw_all, row_send, rows_a, rows_b, stat_all, ports_a, ports_b, port_send,
    coef_seg, coef_mine,
    in_sem, halo_send, halo_recv, fan_send, fan_recv,
):
    nx, ny, nz, zc, yc, wells = dims
    ng = ny * nz
    lines = zc * yc
    pieces = lines // 8
    mx, my, mz = lax.axis_index("gx"), lax.axis_index("gy"), lax.axis_index("gz")
    mg = my * nz + mz

    loads = [
        pltpu.make_async_copy(a, b, in_sem.at[i])
        for i, (a, b) in enumerate(
            (
                (py_in, py), (pz_in, pz), (px_in, px), (st_in, st), (rhs_in, rhs),
                (cell_in, cell_ref), (well_in, well_ref), (wgt_in, wgt_ref), (cnt_in, cnt_ref), (bhp_in, bhp_ref),
            )
        )
    ]
    for load in loads[5:] + loads[:5]:
        load.start()

    barrier = pltpu.get_barrier_semaphore()

    def greet_x(t, c):
        pl.semaphore_signal(barrier, inc=1, device_id={"gx": lax.rem(mx + t, nx)}, device_id_type=MESH)
        return c

    def greet_group(t, c):
        peer = lax.rem(mg + t, ng)
        pl.semaphore_signal(
            barrier, inc=1, device_id={"gy": lax.div(peer, nz), "gz": lax.rem(peer, nz)}, device_id_type=MESH
        )
        return c

    lax.fori_loop(1, ng, greet_group, 0)
    lax.fori_loop(1, nx, greet_x, 0)

    for load in loads[5:]:
        load.wait()
    code = cell_ref[...]
    wellv = well_ref[...]
    wgtv = wgt_ref[...]
    lane8 = lane_of((8, LANES))
    sw_row = jnp.zeros((8, LANES), F32)
    for d in range(ng):
        rows = slice(d * 8, d * 8 + 8)
        c = lane_spread(code, d, (8, LANES))
        w = lane_spread(wgtv, d, (8, LANES))
        x = jnp.bitwise_and(c, LANES - 1)
        hot_x[rows, :] = jnp.where(lane8 == x, 1.0, 0.0)
        mine = jnp.where(lane8 == lane_spread(wellv, d, (8, LANES)) + d * wells, 1.0, 0.0)
        mine = mine * w
        hot_dw[rows, :] = mine
        sw_row = sw_row + mine
    sw_send[0] = jnp.sum(sw_row, axis=0, keepdims=True)
    lane1 = lane_of((1, LANES))
    counts = jnp.zeros((1, LANES), F32)
    bores = jnp.zeros((1, LANES), F32)
    for w in range(wells):
        here = lane1 == mg * wells + w
        counts = jnp.where(here, cnt_ref[0, w].astype(F32), counts)
        bores = jnp.where(here, bhp_ref[0, w], bores)
    sw_send[1] = counts
    sw_send[2] = bores

    def ring(offset, size):
        return min(offset, size - offset)

    group_offsets = [(dy, dz) for dy in range(ny) for dz in range(nz) if (dy, dz) != (0, 0)]
    group_offsets.sort(key=lambda o: -(ring(o[0], ny) + ring(o[1], nz)))
    x_offsets = sorted(range(1, nx), key=lambda o: -ring(o, nx))

    def fan(peers, source, target, which):
        for peer in peers:
            pltpu.make_async_remote_copy(
                src_ref=source, dst_ref=target, send_sem=fan_send.at[which], recv_sem=fan_recv.at[which],
                device_id=peer, device_id_type=MESH,
            ).start()

    def fan_group(source, target, which):
        peers = [{"gy": lax.rem(my + dy, ny), "gz": lax.rem(mz + dz, nz)} for dy, dz in group_offsets]
        fan(peers, source, target.at[mg], which)

    def fan_x(source, target, which):
        fan([{"gx": lax.rem(mx + dx, nx)} for dx in x_offsets], source, target.at[mx], which)

    def fan_wait(target, count, sems, which):
        view = target.at[pl.ds(0, count)]
        pltpu.make_async_copy(view, view, sems.at[which]).wait()

    y_next, y_prev = lax.rem(my + 1, ny), lax.rem(my + ny - 1, ny)
    z_next, z_prev = lax.rem(mz + 1, nz), lax.rem(mz + nz - 1, nz)

    def halo_copy(source, target, which, peer):
        return pltpu.make_async_remote_copy(
            src_ref=source, dst_ref=target, send_sem=halo_send.at[which], recv_sem=halo_recv.at[which],
            device_id=peer, device_id_type=MESH,
        )

    def halos(y_src, y_dst, z_src, z_dst, base):
        last = pl.ds((zc - 1) * yc, yc)
        return [
            halo_copy(y_src.at[0], y_dst.at[1], base, {"gy": y_prev}),
            halo_copy(y_src.at[1], y_dst.at[0], base + 1, {"gy": y_next}),
            halo_copy(z_src.at[pl.ds(0, yc)], z_dst.at[1], base + 2, {"gz": z_prev}),
            halo_copy(z_src.at[last], z_dst.at[0], base + 3, {"gz": z_next}),
        ]

    loads[0].wait()
    loads[1].wait()
    for z in range(zc):
        ysend_perm[0, z] = py[z * yc : z * yc + 1, :]
        ysend_perm[1, z] = py[z * yc + yc - 1 : z * yc + yc, :]

    pl.semaphore_wait(barrier, ng - 1 + nx - 1)
    fan_group(sw_send, sw_all, 0)
    perm_halos = halos(ysend_perm, yperm, pz, zperm, 0)
    for copy in perm_halos:
        copy.start()
    sw_all[mg] = sw_send[...]

    for half in range(lines // LANES):
        for d in range(ng):
            line = jnp.right_shift(lane_spread(code, d, (8, LANES)), 7) - half * LANES
            line_sel[d * 8 : d * 8 + 8, half * LANES : half * LANES + LANES] = jnp.where(lane8 == line, 1.0, 0.0)
    line_sel_t[...] = line_sel[...].T.astype(BF16)

    loads[2].wait()
    loads[3].wait()
    lane_s = lane_of((yc, LANES))
    row_s = row_of((yc, LANES))
    for z in range(zc):
        rows = slice(z * yc, z * yc + yc)
        v = px[rows, :]
        f = jnp.where(lane_s == 0, 0.0, harmonic(pltpu.roll(v, 1, 1), v))
        left[rows, :] = f
        right[rows, :] = pltpu.roll(f, LANES - 1, 1)
    for copy in perm_halos:
        copy.wait_recv()
    for z in range(zc):
        rows = slice(z * yc, z * yc + yc)
        v = py[rows, :]
        below = jnp.where(row_s == 0, yperm[0, z], pltpu.roll(v, 1, 0))
        f = harmonic(below, v)
        f = jnp.where(jnp.logical_and(row_s == 0, my == 0), 0.0, f)
        top = harmonic(py[z * yc + yc - 1 : z * yc + yc, :], yperm[1, z])
        top = jnp.where(my == ny - 1, 0.0, top)
        g = jnp.where(row_s == yc - 1, top, pltpu.roll(f, yc - 1, 0))
        ylo[rows, :] = f
        yup[rows, :] = g
        sig[rows, :] = st[rows, :] + f + g
    before = zperm[0]
    for z in range(zc + 1):
        v = pz[z * yc : z * yc + yc, :] if z < zc else zperm[1]
        f = harmonic(before, v)
        if z == 0:
            f = jnp.where(mz == 0, 0.0, f)
        if z == zc:
            f = jnp.where(mz == nz - 1, 0.0, f)
        zface[z * yc : z * yc + yc, :] = f
        before = v
    for z in range(zc):
        rows = slice(z * yc, z * yc + yc)
        sig[rows, :] = sig[rows, :] + zface[rows, :] + zface[z * yc + yc : z * yc + 2 * yc, :]

    chunk = 64
    lane_c = lane_of((chunk, LANES))
    strides = [1 << i for i in range(7)]

    def reduce_matrix(i, carry):
        rows = pl.ds(pl.multiple_of(i * chunk, chunk), chunk)
        lo, hi, s = left[rows, :], right[rows, :], sig[rows, :]
        for level, stride in enumerate(strides):
            r = 1.0 / (s + lo + hi)
            from_low = lane_c > stride
            from_high = lane_c < LANES - 1 - stride
            a = jnp.where(from_low, lo * pltpu.roll(r, stride, 1), 0.0)
            g = jnp.where(from_high, hi * pltpu.roll(r, LANES - stride, 1), 0.0)
            s = s + a * pltpu.roll(s, stride, 1) + g * pltpu.roll(s, LANES - stride, 1)
            lo = jnp.where(from_low, a * pltpu.roll(lo, stride, 1), lo)
            hi = jnp.where(from_high, g * pltpu.roll(hi, LANES - stride, 1), hi)
            alpha[level, rows, :] = a
            gamma[level, rows, :] = g
        r = 1.0 / (s + lo + hi)
        first, last = lane_c == 0, lane_c == LANES - 1
        end = jnp.logical_or(first, last)
        inv[rows, :] = jnp.where(end, 0.0, r)
        low_w[rows, :] = jnp.where(first, 1.0, jnp.where(last, 0.0, lo * r))
        high_w[rows, :] = jnp.where(last, 1.0, jnp.where(first, 0.0, hi * r))
        sig[rows, :] = s
        right[rows, :] = hi
        return carry

    lax.fori_loop(0, lines // chunk, reduce_matrix, 0)

    def ends_of(ref):
        return pack_ends([ref[j * 8 : j * 8 + 8, :] for j in range(pieces)])

    stat_all[mx, 0] = ends_of(sig) + pltpu.roll(ends_of(px), LANES // 2, 1)
    stat_all[mx, 1] = ends_of(right)
    fan_x(stat_all.at[mx], stat_all, 1)

    fan_wait(sw_all, ng - 1, fan_recv, 0)
    total = jnp.zeros((3, 1, LANES), F32)
    for s in range(ng):
        total = total + sw_all[s]
    count, bore = total[1], total[2]

    def slot_of(g):
        return jnp.floor(g * count * (1.0 / nz))

    layer_slots = [slot_of(float(g)) for g in range(nz)]
    layer_sw = [sum(sw_all[y * nz + g, 0] for y in range(ny)) for g in range(nz)]
    layer_inv = []
    layer_seg = []
    for g in range(nz):
        same = sum(jnp.where(layer_slots[h] == layer_slots[g], layer_sw[h], 0.0) for h in range(nz))
        layer_seg.append(same)
        layer_inv.append(1.0 / (same + BORE))
    my_slot = slot_of(mz.astype(F32))
    my_inv = jnp.zeros((1, LANES), F32)
    for g in range(nz):
        my_inv = jnp.where(mz == g, layer_inv[g], my_inv)
    for g in range(nz):
        coef_seg[g] = layer_inv[g]
        coef_mine[g] = jnp.where(layer_slots[g] == my_slot, 1.0, 0.0) * my_inv
    my_base = BORE * bore * my_inv

    def well_sources(pressure_cols, seg_row):
        drop = seg_row if pressure_cols is None else seg_row - pressure_cols
        back = jnp.sum(hot_dw[...] * drop, axis=1, keepdims=True)
        return onehot_product(line_sel_t[...], hot_x[...] * back)

    def solve_local(b_ref):
        half = lines // 2
        ends = []
        for h in range(2):
            rows = slice(h * half, h * half + half)
            b = b_ref[rows, :]
            for level, stride in enumerate(strides):
                b = b + alpha[level, rows, :] * pltpu.roll(b, stride, 1) + gamma[level, rows, :] * pltpu.roll(
                    b, LANES - stride, 1
                )
            b_ref[rows, :] = b
            ends += [b[j * 8 : j * 8 + 8, :] for j in range(half // 8)]
        packed = pack_ends(ends)
        return packed + pltpu.roll(packed, LANES // 2, 1)

    loads[4].wait()
    src[...] = rhs[...] + well_sources(None, my_base)
    ports_a[mx] = solve_local(src)
    fan_x(ports_a.at[mx], ports_a, 2)

    fan_wait(stat_all, nx - 1, fan_recv, 1)

    def ends_at(k):
        s, c = stat_all[k, 0], stat_all[k, 1]
        return dict(
            sz=s, sf=pltpu.roll(s, LANES - 1, 1), pz=pltpu.roll(s, LANES // 2, 1),
            pf=pltpu.roll(s, LANES // 2 - 1, 1), c=pltpu.roll(c, LANES - 1, 1),
        )

    own = ends_at(mx)

    def walk(direction):
        chain = []
        for t in range(1, nx):
            k = mx + direction * t
            valid = jnp.logical_and(k >= 0, k < nx)
            chain.append((jnp.clip(k, 0, nx - 1), valid))
        blocks = [ends_at(k) for k, _ in chain]
        ground = jnp.zeros((8, LANES), F32)
        factors = [None] * (nx - 1)
        for t in range(nx - 1, 0, -1):
            b = blocks[t - 1]
            nearer = own if t == 1 else blocks[t - 2]
            far, near, edge = ("sf", "sz", ("pz", "pf")) if direction < 0 else ("sz", "sf", ("pf", "pz"))
            face = jnp.where(chain[t - 1][1], harmonic(b[edge[0]], nearer[edge[1]]), 0.0)
            through = b["c"] / (b["c"] + b[far] + ground)
            inner = b[near] + (b[far] + ground) * through
            outward = face / (face + inner)
            ground = inner * outward
            factors[t - 1] = (through, outward)
        reach = jnp.ones((8, LANES), F32)
        weights = []
        for through, outward in factors:
            near_w = reach * outward
            reach = near_w * through
            weights.append((near_w, reach))
        return ground, weights, [k for k, _ in chain]

    ground_l, weights_l, index_l = walk(-1)
    ground_r, weights_r, index_r = walk(1)
    a, e, c = own["sf"] + ground_l, own["sz"] + ground_r, own["c"]
    scale = 1.0 / (a * e + (a + e) * c)
    ff, fz, zz = (e + c) * scale, c * scale, (a + c) * scale
    even = lane8 % 2 == 0
    lower_half = lane8 < LANES // 2

    def weave(z_first, f_first, z_last, f_last):
        first = jnp.where(even, z_first, pltpu.roll(f_first, 1, 1))
        last = jnp.where(even, pltpu.roll(z_last, LANES // 2, 1), pltpu.roll(f_last, LANES // 2 + 1, 1))
        return jnp.where(lower_half, first, last)

    terms = [(mx, weave(fz, ff, zz, fz))]
    for (near_w, far_w), k in zip(weights_l, index_l):
        terms.append((k, weave(ff * near_w, ff * far_w, fz * near_w, fz * far_w)))
    for (near_w, far_w), k in zip(weights_r, index_r):
        terms.append((k, weave(fz * far_w, fz * near_w, zz * far_w, zz * near_w)))

    def join(ports, b_ref, target):
        ends = sum(w * ports[k] for k, w in terms)
        ends = ends + pltpu.roll(ends, LANES - 1, 1)
        for j in range(pieces):
            rows = slice(j * 8, j * 8 + 8)
            first = lane_spread(ends, 2 * j, (8, LANES))
            last = lane_spread(ends, LANES // 2 + 2 * j, (8, LANES))
            target[rows, :] = b_ref[rows, :] * inv[rows, :] + low_w[rows, :] * first + high_w[rows, :] * last

    def perforated(values):
        rows = onehot_product(line_sel[...].astype(BF16), values[...])
        cols = jnp.sum(rows * hot_x[...], axis=1, keepdims=True)
        return cols, jnp.sum(hot_dw[...] * cols, axis=0, keepdims=True)

    fan_wait(ports_a, nx - 1, fan_recv, 2)

    join(ports_a, src, field)
    for z in range(zc):
        ysend_p[0, z] = field[z * yc : z * yc + 1, :]
        ysend_p[1, z] = field[z * yc + yc - 1 : z * yc + yc, :]
    p_halos = halos(ysend_p, yp, field, zp, 4)
    for copy in p_halos:
        copy.start()
    cols, row = perforated(field)
    row_send[0] = row
    fan_group(row_send.at[0], rows_a, 3)
    rows_a[mg] = row

    for copy in p_halos:
        copy.wait_recv()
    for z in range(zc):
        rows = slice(z * yc, z * yc + yc)
        v = field[rows, :]
        below = jnp.where(row_s == 0, yp[0, z], pltpu.roll(v, 1, 0))
        above = jnp.where(row_s == yc - 1, yp[1, z], pltpu.roll(v, yc - 1, 0))
        under = field[z * yc - yc : z * yc, :] if z > 0 else zp[0]
        over = field[z * yc + yc : z * yc + 2 * yc, :] if z < zc - 1 else zp[1]
        beside = ylo[rows, :] * below + yup[rows, :] * above
        beside = beside + zface[rows, :] * under + zface[z * yc + yc : z * yc + 2 * yc, :] * over
        src[rows, :] = rhs[rows, :] + beside

    fan_wait(rows_a, ng - 1, fan_recv, 3)
    seg_row = my_base
    for g in range(nz):
        seg_row = seg_row + coef_mine[g] * sum(rows_a[y * nz + g] for y in range(ny))
    src[...] = src[...] + well_sources(cols, seg_row)

    ports_b[mx] = solve_local(src)
    fan_x(ports_b.at[mx], ports_b, 4)
    fan_wait(ports_b, nx - 1, fan_recv, 4)

    join(ports_b, src, p_out)
    _, row = perforated(p_out)
    row_send[1] = row
    fan_group(row_send.at[1], rows_b, 5)
    rows_b[mg] = row
    fan_wait(rows_b, ng - 1, fan_recv, 5)
    res = jnp.zeros((1, LANES), F32)
    for g in range(nz):
        inflow = sum(rows_b[y * nz + g] - bore * sw_all[y * nz + g, 0] for y in range(ny))
        res = res + coef_seg[g] * inflow
    res_out[...] = pltpu.roll(res, lax.rem(LANES - mg * wells, LANES), 1)[:, :wells]

    for copy in perm_halos + p_halos:
        copy.wait_send()
    fan_wait(sw_all, ng - 1, fan_send, 0)
    fan_wait(stat_all, nx - 1, fan_send, 1)
    fan_wait(ports_a, nx - 1, fan_send, 2)
    fan_wait(rows_a, ng - 1, fan_send, 3)
    fan_wait(ports_b, nx - 1, fan_send, 4)
    fan_wait(rows_b, ng - 1, fan_send, 5)


def shards(dims, rhs, perm_x, perm_y, perm_z, storage, perf_cell, perf_well, perf_index, seg_count, bhp):
    nx, ny, nz, zc, yc, wells = dims
    ng = ny * nz
    lines = zc * yc
    perfs = ng * 8
    plane = (lines, LANES)
    flat = [a.reshape(plane) for a in (rhs, perm_x, perm_y, perm_z, storage)]
    slots = [a[0, 0].T for a in (perf_cell, perf_well, perf_index)]
    operands = [pltpu.with_memory_space_constraint(a, pltpu.HBM) for a in (*slots, seg_count[0], bhp[0], *flat)]
    vmem = pl.BlockSpec(memory_space=pltpu.VMEM)
    hbm = pl.BlockSpec(memory_space=pltpu.HBM)
    whole = pltpu.VMEM(plane, F32)
    perf_plane = pltpu.VMEM((perfs, LANES), F32)
    pressure, residual = pl.pallas_call(
        functools.partial(kernel, dims),
        out_shape=(pltpu.VMEM(plane, F32), pltpu.VMEM((1, wells), F32)),
        in_specs=[hbm] * 10,
        out_specs=(vmem, vmem),
        scratch_shapes=[pltpu.VMEM((8, ng), jnp.int32)] * 2
        + [pltpu.VMEM((8, ng), F32), pltpu.SMEM((1, wells), jnp.int32), pltpu.SMEM((1, wells), F32)]
        + [whole] * 5
        + [whole] * 5
        + [pltpu.VMEM((lines + yc, LANES), F32)]
        + [pltpu.VMEM((7, lines, LANES), F32)] * 2
        + [whole] * 5
        + [perf_plane] * 2
        + [pltpu.VMEM((perfs, lines), F32), pltpu.VMEM((lines, perfs), BF16)]
        + [pltpu.VMEM((2, zc, 1, LANES), F32), pltpu.VMEM((2, yc, LANES), F32)]
        + [pltpu.VMEM((2, zc, 1, LANES), F32)] * 3
        + [pltpu.VMEM((2, yc, LANES), F32)]
        + [pltpu.VMEM((3, 1, LANES), F32), pltpu.VMEM((ng, 3, 1, LANES), F32)]
        + [pltpu.VMEM((2, 1, LANES), F32)]
        + [pltpu.VMEM((ng, 1, LANES), F32)] * 2
        + [pltpu.VMEM((nx, 2, 8, LANES), F32)]
        + [pltpu.VMEM((nx, 8, LANES), F32)] * 2
        + [pltpu.VMEM((8, LANES), F32)]
        + [pltpu.VMEM((nz, 1, LANES), F32)] * 2
        + [
            pltpu.SemaphoreType.DMA((10,)),
            pltpu.SemaphoreType.DMA((8,)),
            pltpu.SemaphoreType.DMA((8,)),
            pltpu.SemaphoreType.DMA((6,)),
            pltpu.SemaphoreType.DMA((6,)),
        ],
        compiler_params=pltpu.CompilerParams(
            collective_id=0, has_side_effects=True, vmem_limit_bytes=32 * 1024 * 1024
        ),
        name="sweeps",
    )(*operands)
    return pressure.reshape(rhs.shape), residual.reshape(1, 1, wells)


def solution(mesh):
    nx, ny, nz = mesh.shape["gx"], mesh.shape["gy"], mesh.shape["gz"]
    cells = P("gz", "gy", "gx")
    perfs = P("gx", ("gy", "gz"), None, None)
    owned = P("gx", ("gy", "gz"), None)

    def program(rhs, perm_x, perm_y, perm_z, storage, perf_cell, perf_well, perf_index, seg_count, bhp):
        dims = (nx, ny, nz, rhs.shape[0] // nz, rhs.shape[1] // ny, seg_count.shape[-1])
        return jax.shard_map(
            functools.partial(shards, dims),
            mesh=mesh,
            in_specs=(cells,) * 5 + (perfs,) * 3 + (owned,) * 2,
            out_specs=(cells, owned),
            check_vma=False,
        )(rhs, perm_x, perm_y, perm_z, storage, perf_cell, perf_well, perf_index, seg_count, bhp)

    return program
```

```python
import functools

import jax
import jax.numpy as jnp
from jax import lax
from jax.experimental import pallas as pl
from jax.experimental.pallas import tpu as pltpu
from jax.sharding import PartitionSpec as P

F32 = jnp.float32
BF16 = jnp.bfloat16
MESH = pl.DeviceIdType.MESH
LANES = 128
SEG = 4
BORE = 20.0


def harmonic(a, b):
    return 2.0 * a * b / (a + b)


def lane_of(shape):
    return lax.broadcasted_iota(jnp.int32, shape, len(shape) - 1)


def row_of(shape):
    return lax.broadcasted_iota(jnp.int32, shape, len(shape) - 2)


def split_lanes(x):
    high = x.astype(BF16)
    low = (x - high.astype(F32)).astype(BF16)
    return jnp.concatenate([high, low], axis=1)


def onehot_product(selector, x):
    both = jnp.dot(selector, split_lanes(x), preferred_element_type=F32)
    return both[:, :LANES] + both[:, LANES:]


def lane_spread(x, lane, shape):
    return jnp.broadcast_to(x[:, lane : lane + 1], shape)


def pack_ends(pieces):
    pair = lane_of((8, LANES)) // 2
    packed = jnp.zeros((8, LANES), F32)
    for j, piece in enumerate(pieces):
        packed = jnp.where(pair == j, pltpu.roll(piece, 2 * j + 1, 1), packed)
    return packed


def kernel(
    dims, cell_in, well_in, wgt_in, cnt_in, bhp_in, rhs_in, px_in, py_in, pz_in, st_in, p_out, res_out,
    cell_ref, well_ref, wgt_ref, cnt_ref, bhp_ref, rhs, px, py, pz, st,
    sig, left, right, ylo, yup, zface, low_m, high_m, recip, inv, low_w, high_w, src, field,
    hot_x, hot_dw, line_sel, line_sel_t, reach_first, reach_last,
    yperm, zperm, yp, ysend_perm, ysend_p, zp,
    sw_send, sw_all, row_send, rows_a, rows_b, stat_all, ports_a, ports_b,
    in_sem, halo_send, halo_recv, fan_send, fan_recv,
):
    nx, ny, nz, zc, yc, wells = dims
    ng = ny * nz
    lines = zc * yc
    pieces = lines // 8
    mx, my, mz = lax.axis_index("gx"), lax.axis_index("gy"), lax.axis_index("gz")
    mg = my * nz + mz

    def ring(offset, size):
        return min(offset, size - offset)

    group_offsets = [(dy, dz) for dy in range(ny) for dz in range(nz) if (dy, dz) != (0, 0)]
    group_offsets.sort(key=lambda o: -(ring(o[0], ny) + ring(o[1], nz)))
    group_peers = [{"gy": lax.rem(my + dy, ny), "gz": lax.rem(mz + dz, nz)} for dy, dz in group_offsets]
    x_offsets = sorted(range(1, nx), key=lambda o: -ring(o, nx))
    x_peers = [{"gx": lax.rem(mx + dx, nx)} for dx in x_offsets]

    barrier = pltpu.get_barrier_semaphore()
    for peer in group_peers + x_peers:
        pl.semaphore_signal(barrier, inc=1, device_id=peer, device_id_type=MESH)

    loads = [
        pltpu.make_async_copy(a, b, in_sem.at[i])
        for i, (a, b) in enumerate(
            (
                (py_in, py), (pz_in, pz), (px_in, px), (st_in, st), (rhs_in, rhs),
                (cell_in, cell_ref), (well_in, well_ref), (wgt_in, wgt_ref), (cnt_in, cnt_ref), (bhp_in, bhp_ref),
            )
        )
    ]
    for load in loads[5:] + loads[:5]:
        load.start()

    def fan(peers, source, target, which):
        for peer in peers:
            pltpu.make_async_remote_copy(
                src_ref=source, dst_ref=target, send_sem=fan_send.at[which], recv_sem=fan_recv.at[which],
                device_id=peer, device_id_type=MESH,
            ).start()

    def fan_wait(target, count, sems, which):
        view = target.at[pl.ds(0, count)]
        pltpu.make_async_copy(view, view, sems.at[which]).wait()

    y_next, y_prev = lax.rem(my + 1, ny), lax.rem(my + ny - 1, ny)
    z_next, z_prev = lax.rem(mz + 1, nz), lax.rem(mz + nz - 1, nz)

    def halos(y_src, y_dst, z_src, z_dst, base):
        last = pl.ds((zc - 1) * yc, yc)
        routes = (
            (y_src.at[0], y_dst.at[1], {"gy": y_prev}),
            (y_src.at[1], y_dst.at[0], {"gy": y_next}),
            (z_src.at[pl.ds(0, yc)], z_dst.at[1], {"gz": z_prev}),
            (z_src.at[last], z_dst.at[0], {"gz": z_next}),
        )
        return [
            pltpu.make_async_remote_copy(
                src_ref=a, dst_ref=b, send_sem=halo_send.at[base + i], recv_sem=halo_recv.at[base + i],
                device_id=peer, device_id_type=MESH,
            )
            for i, (a, b, peer) in enumerate(routes)
        ]

    for load in loads[5:]:
        load.wait()
    code = cell_ref[...]
    wellv = well_ref[...]
    wgtv = wgt_ref[...]
    piece = (8, LANES)
    lane8 = lane_of(piece)
    sw_row = jnp.zeros(piece, F32)
    for d in range(ng):
        mine = lane8 == lane_spread(wellv, d, piece) + d * wells
        mine = jnp.where(mine, lane_spread(wgtv, d, piece), 0.0)
        hot_dw[d * 8 : d * 8 + 8, :] = mine
        sw_row = sw_row + mine
    sw_send[0] = jnp.sum(sw_row, axis=0, keepdims=True)
    lane1 = lane_of((1, LANES))
    counts = jnp.zeros((1, LANES), F32)
    bores = jnp.zeros((1, LANES), F32)
    for w in range(wells):
        here = lane1 == mg * wells + w
        counts = jnp.where(here, cnt_ref[0, w].astype(F32), counts)
        bores = jnp.where(here, bhp_ref[0, w], bores)
    sw_send[1] = counts
    sw_send[2] = bores

    loads[0].wait()
    loads[1].wait()
    for z in range(zc):
        ysend_perm[0, z] = py[z * yc : z * yc + 1, :]
        ysend_perm[1, z] = py[z * yc + yc - 1 : z * yc + yc, :]

    pl.semaphore_wait(barrier, ng - 1 + nx - 1)
    perm_halos = halos(ysend_perm, yperm, pz, zperm, 0)
    for copy in perm_halos:
        copy.start()
    fan(group_peers, sw_send, sw_all.at[mg], 0)
    sw_all[mg] = sw_send[...]

    loads[2].wait()
    loads[3].wait()
    lane_s = lane_of((yc, LANES))
    row_s = row_of((yc, LANES))
    for z in range(zc):
        rows = slice(z * yc, z * yc + yc)
        v = px[rows, :]
        f = jnp.where(lane_s == 0, 0.0, harmonic(pltpu.roll(v, 1, 1), v))
        left[rows, :] = f
        right[rows, :] = pltpu.roll(f, LANES - 1, 1)
        v = py[rows, :]
        f = harmonic(pltpu.roll(v, 1, 0), v)
        ylo[rows, :] = f
        if z > 0:
            zface[rows, :] = harmonic(pz[z * yc - yc : z * yc, :], pz[rows, :])
    for copy in perm_halos:
        copy.wait_recv()
    zface[0:yc, :] = jnp.where(mz == 0, 0.0, harmonic(zperm[0], pz[0:yc, :]))
    zface[lines : lines + yc, :] = jnp.where(mz == nz - 1, 0.0, harmonic(pz[lines - yc : lines, :], zperm[1]))
    for z in range(zc):
        rows = slice(z * yc, z * yc + yc)
        low = jnp.where(my == 0, 0.0, harmonic(yperm[0, z], py[z * yc : z * yc + 1, :]))
        top = jnp.where(my == ny - 1, 0.0, harmonic(py[z * yc + yc - 1 : z * yc + yc, :], yperm[1, z]))
        f = jnp.where(row_s == 0, low, ylo[rows, :])
        g = jnp.where(row_s == yc - 1, top, pltpu.roll(f, yc - 1, 0))
        ylo[rows, :] = f
        yup[rows, :] = g
        sig[rows, :] = st[rows, :] + f + g + zface[rows, :] + zface[z * yc + yc : z * yc + 2 * yc, :]

    chunk = 128
    lane_c = lane_of((chunk, LANES))
    strides = [1 << i for i in range(7)]

    def reduce_matrix(i, carry):
        rows = pl.ds(pl.multiple_of(i * chunk, chunk), chunk)
        lo, hi, s = left[rows, :], right[rows, :], sig[rows, :]
        for level, stride in enumerate(strides):
            r = 1.0 / (s + lo + hi)
            from_low = lane_c > stride
            from_high = lane_c < LANES - 1 - stride
            a = jnp.where(from_low, lo, 0.0)
            g = jnp.where(from_high, hi, 0.0)
            low_m[level, rows, :] = a
            high_m[level, rows, :] = g
            recip[level, rows, :] = r
            q = s * r
            s = s + a * pltpu.roll(q, stride, 1) + g * pltpu.roll(q, LANES - stride, 1)
            lo = jnp.where(from_low, lo * pltpu.roll(lo * r, stride, 1), lo)
            hi = jnp.where(from_high, hi * pltpu.roll(hi * r, LANES - stride, 1), hi)
        r = 1.0 / (s + lo + hi)
        first, last = lane_c == 0, lane_c == LANES - 1
        inv[rows, :] = jnp.where(jnp.logical_or(first, last), 0.0, r)
        low_w[rows, :] = jnp.where(first, 1.0, jnp.where(last, 0.0, lo * r))
        high_w[rows, :] = jnp.where(last, 1.0, jnp.where(first, 0.0, hi * r))
        sig[rows, :] = s
        right[rows, :] = hi
        return carry

    lax.fori_loop(0, lines // chunk, reduce_matrix, 0)

    def ends_of(ref):
        return pack_ends([ref[j * 8 : j * 8 + 8, :] for j in range(pieces)])

    stat_all[mx, 0] = ends_of(sig) + pltpu.roll(ends_of(px), LANES // 2, 1)
    stat_all[mx, 1] = ends_of(right)
    fan(x_peers, stat_all.at[mx], stat_all.at[mx], 1)

    for d in range(ng):
        c = lane_spread(code, d, piece)
        rows = slice(d * 8, d * 8 + 8)
        hot_x[rows, :] = jnp.where(lane8 == jnp.bitwise_and(c, LANES - 1), 1.0, 0.0)
        for half in range(lines // LANES):
            hit = lane8 == jnp.right_shift(c, 7) - half * LANES
            line_sel[rows, half * LANES : half * LANES + LANES] = jnp.where(hit, 1.0, 0.0)
    line_sel_t[...] = line_sel[...].T.astype(BF16)

    def at_perforations(values):
        rows = onehot_product(line_sel[...].astype(BF16), values)
        return jnp.sum(rows * hot_x[...], axis=1, keepdims=True)

    reach_first[...] = onehot_product(line_sel_t[...], hot_dw[...] * at_perforations(low_w[...]))
    reach_last[...] = onehot_product(line_sel_t[...], hot_dw[...] * at_perforations(high_w[...]))

    pair8 = lane8 // 2
    even = lane8 % 2 == 0

    def line_ends(for_first, for_last):
        packed = jnp.zeros(piece, F32)
        for j in range(pieces):
            rows = slice(j * 8, j * 8 + 8)
            both = jnp.where(
                even,
                jnp.sum(for_last(rows), axis=1, keepdims=True),
                jnp.sum(for_first(rows), axis=1, keepdims=True),
            )
            packed = jnp.where(pair8 == j, both, packed)
        return packed

    def end_sources(values):
        return line_ends(lambda rows: low_w[rows, :] * values[rows, :], lambda rows: high_w[rows, :] * values[rows, :])

    def end_wells(seg_row):
        return line_ends(lambda rows: reach_first[rows, :] * seg_row, lambda rows: reach_last[rows, :] * seg_row)

    def send_ports(ports, packed, which):
        ports[mx] = packed + pltpu.roll(packed, LANES // 2, 1)
        fan(x_peers, ports.at[mx], ports.at[mx], which)

    def well_field(drop):
        back = jnp.sum(hot_dw[...] * drop, axis=1, keepdims=True)
        return onehot_product(line_sel_t[...], hot_x[...] * back)

    def solve_local():
        half = lines // 2
        for h in range(2):
            rows = slice(h * half, h * half + half)
            b = src[rows, :]
            for level, stride in enumerate(strides):
                t = b * recip[level, rows, :]
                b = b + low_m[level, rows, :] * pltpu.roll(t, stride, 1) + high_m[level, rows, :] * pltpu.roll(
                    t, LANES - stride, 1
                )
            src[rows, :] = b * inv[rows, :]

    def well_sums(cols):
        return jnp.sum(hot_dw[...] * cols, axis=0, keepdims=True)

    loads[4].wait()
    ends_rhs = end_sources(rhs)

    fan_wait(sw_all, ng - 1, fan_recv, 0)
    layer_all = [sum(sw_all[y * nz + g] for y in range(ny)) for g in range(nz)]
    total = sum(layer_all)
    count, bore = total[1], total[2]
    layer_sw = [layer[0] for layer in layer_all]

    def slot_of(g):
        return jnp.floor(g * count * (1.0 / nz))

    my_slot = slot_of(mz.astype(F32))
    layer_slots = [slot_of(float(g)) for g in range(nz)]
    same = [jnp.where(slot == my_slot, 1.0, 0.0) for slot in layer_slots]
    my_inv = 1.0 / (sum(m * sw for m, sw in zip(same, layer_sw)) + BORE)
    my_base = BORE * bore * my_inv
    send_ports(ports_a, ends_rhs + end_wells(my_base), 2)

    fan_wait(stat_all, nx - 1, fan_recv, 1)

    def ends_at(k):
        s, c = stat_all[k, 0], stat_all[k, 1]
        return dict(
            sz=s, sf=pltpu.roll(s, LANES - 1, 1), pz=pltpu.roll(s, LANES // 2, 1),
            pf=pltpu.roll(s, LANES // 2 - 1, 1), c=pltpu.roll(c, LANES - 1, 1),
        )

    own = ends_at(mx)

    def walk(direction):
        chain = []
        for t in range(1, nx):
            k = mx + direction * t
            valid = jnp.logical_and(k >= 0, k < nx)
            chain.append((jnp.clip(k, 0, nx - 1), valid))
        blocks = [ends_at(k) for k, _ in chain]
        ground = jnp.zeros(piece, F32)
        factors = [None] * (nx - 1)
        for t in range(nx - 1, 0, -1):
            b = blocks[t - 1]
            nearer = own if t == 1 else blocks[t - 2]
            far, near, edge = ("sf", "sz", ("pz", "pf")) if direction < 0 else ("sz", "sf", ("pf", "pz"))
            face = jnp.where(chain[t - 1][1], harmonic(b[edge[0]], nearer[edge[1]]), 0.0)
            through = b["c"] / (b["c"] + b[far] + ground)
            inner = b[near] + (b[far] + ground) * through
            outward = face / (face + inner)
            ground = inner * outward
            factors[t - 1] = (through, outward)
        reach = jnp.ones(piece, F32)
        weights = []
        for through, outward in factors:
            near_w = reach * outward
            reach = near_w * through
            weights.append((near_w, reach))
        return ground, weights, [k for k, _ in chain]

    ground_l, weights_l, index_l = walk(-1)
    ground_r, weights_r, index_r = walk(1)
    a, e, c = own["sf"] + ground_l, own["sz"] + ground_r, own["c"]
    scale = 1.0 / (a * e + (a + e) * c)
    ff, fz, zz = (e + c) * scale, c * scale, (a + c) * scale
    lower_half = lane8 < LANES // 2

    def weave(z_first, f_first, z_last, f_last):
        first = jnp.where(even, z_first, pltpu.roll(f_first, 1, 1))
        last = jnp.where(even, pltpu.roll(z_last, LANES // 2, 1), pltpu.roll(f_last, LANES // 2 + 1, 1))
        return jnp.where(lower_half, first, last)

    terms = [(mx, weave(fz, ff, zz, fz))]
    for (near_w, far_w), k in zip(weights_l, index_l):
        terms.append((k, weave(ff * near_w, ff * far_w, fz * near_w, fz * far_w)))
    for (near_w, far_w), k in zip(weights_r, index_r):
        terms.append((k, weave(fz * far_w, fz * near_w, zz * far_w, zz * near_w)))

    def end_pressures(ports):
        ends = sum(w * ports[k] for k, w in terms)
        ends = ends + pltpu.roll(ends, LANES - 1, 1)
        return [
            (lane_spread(ends, 2 * j, piece), lane_spread(ends, LANES // 2 + 2 * j, piece)) for j in range(pieces)
        ]

    def end_sums(ends):
        given = jnp.zeros(piece, F32)
        for j, (first, last) in enumerate(ends):
            rows = slice(j * 8, j * 8 + 8)
            given = given + reach_first[rows, :] * first + reach_last[rows, :] * last
        return jnp.sum(given, axis=0, keepdims=True)

    def join(ends, target):
        for j, (first, last) in enumerate(ends):
            rows = slice(j * 8, j * 8 + 8)
            target[rows, :] = src[rows, :] + low_w[rows, :] * first + high_w[rows, :] * last

    def send_row(which, row, target):
        row_send[which] = row
        fan(group_peers, row_send.at[which], target.at[mg], 3 + which)
        target[mg] = row

    src[...] = rhs[...] + well_field(my_base)
    solve_local()
    row_own = well_sums(at_perforations(src[...]))
    fan_wait(ports_a, nx - 1, fan_recv, 2)
    ends = end_pressures(ports_a)
    send_row(0, row_own + end_sums(ends), rows_a)

    join(ends, field)
    for z in range(zc):
        ysend_p[0, z] = field[z * yc : z * yc + 1, :]
        ysend_p[1, z] = field[z * yc + yc - 1 : z * yc + yc, :]
    p_halos = halos(ysend_p, yp, field, zp, 4)
    for copy in p_halos:
        copy.start()
    cols = at_perforations(field[...])
    coef_mine = [m * my_inv for m in same]
    coef_seg = []
    for g in range(nz):
        slot_sw = sum(jnp.where(layer_slots[h] == layer_slots[g], layer_sw[h], 0.0) for h in range(nz))
        coef_seg.append(1.0 / (slot_sw + BORE))
    residual_base = bore * sum(f * sw for f, sw in zip(coef_seg, layer_sw))

    for copy in p_halos:
        copy.wait_recv()
    for z in range(zc):
        rows = slice(z * yc, z * yc + yc)
        v = field[rows, :]
        below = jnp.where(row_s == 0, yp[0, z], pltpu.roll(v, 1, 0))
        above = jnp.where(row_s == yc - 1, yp[1, z], pltpu.roll(v, yc - 1, 0))
        under = field[z * yc - yc : z * yc, :] if z > 0 else zp[0]
        over = field[z * yc + yc : z * yc + 2 * yc, :] if z < zc - 1 else zp[1]
        beside = ylo[rows, :] * below + yup[rows, :] * above
        beside = beside + zface[rows, :] * under + zface[z * yc + yc : z * yc + 2 * yc, :] * over
        src[rows, :] = rhs[rows, :] + beside
    src[...] = src[...] + well_field(my_base - cols)
    ends_base = end_sources(src)

    fan_wait(rows_a, ng - 1, fan_recv, 3)
    inflow = sum(f * sum(rows_a[y * nz + g] for y in range(ny)) for g, f in enumerate(coef_mine))
    send_ports(ports_b, ends_base + end_wells(inflow), 5)
    src[...] = src[...] + well_field(inflow)
    solve_local()
    row_own = well_sums(at_perforations(src[...]))
    fan_wait(ports_b, nx - 1, fan_recv, 5)
    ends = end_pressures(ports_b)
    send_row(1, row_own + end_sums(ends), rows_b)
    join(ends, p_out)
    fan_wait(rows_b, ng - 1, fan_recv, 4)
    res = sum(f * sum(rows_b[y * nz + g] for y in range(ny)) for g, f in enumerate(coef_seg)) - residual_base
    res_out[...] = pltpu.roll(res, lax.rem(LANES - mg * wells, LANES), 1)[:, :wells]

    for copy in perm_halos + p_halos:
        copy.wait_send()
    fan_wait(sw_all, ng - 1, fan_send, 0)
    fan_wait(stat_all, nx - 1, fan_send, 1)
    fan_wait(ports_a, nx - 1, fan_send, 2)
    fan_wait(rows_a, ng - 1, fan_send, 3)
    fan_wait(rows_b, ng - 1, fan_send, 4)
    fan_wait(ports_b, nx - 1, fan_send, 5)


def shards(dims, rhs, perm_x, perm_y, perm_z, storage, perf_cell, perf_well, perf_index, seg_count, bhp):
    nx, ny, nz, zc, yc, wells = dims
    ng = ny * nz
    lines = zc * yc
    perfs = ng * 8
    plane = (lines, LANES)
    flat = [a.reshape(plane) for a in (rhs, perm_x, perm_y, perm_z, storage)]
    slots = [a[0, 0].T for a in (perf_cell, perf_well, perf_index)]
    operands = [pltpu.with_memory_space_constraint(a, pltpu.HBM) for a in (*slots, seg_count[0], bhp[0], *flat)]
    vmem = pl.BlockSpec(memory_space=pltpu.VMEM)
    hbm = pl.BlockSpec(memory_space=pltpu.HBM)
    whole = pltpu.VMEM(plane, F32)
    perf_plane = pltpu.VMEM((perfs, LANES), F32)
    pressure, residual = pl.pallas_call(
        functools.partial(kernel, dims),
        out_shape=(pltpu.VMEM(plane, F32), pltpu.VMEM((1, wells), F32)),
        in_specs=[hbm] * 10,
        out_specs=(vmem, vmem),
        scratch_shapes=[pltpu.VMEM((8, ng), jnp.int32)] * 2
        + [pltpu.VMEM((8, ng), F32), pltpu.SMEM((1, wells), jnp.int32), pltpu.SMEM((1, wells), F32)]
        + [whole] * 5
        + [whole] * 5
        + [pltpu.VMEM((lines + yc, LANES), F32)]
        + [pltpu.VMEM((7, lines, LANES), F32)] * 3
        + [whole] * 5
        + [perf_plane] * 2
        + [pltpu.VMEM((perfs, lines), F32), pltpu.VMEM((lines, perfs), BF16)]
        + [whole] * 2
        + [pltpu.VMEM((2, zc, 1, LANES), F32), pltpu.VMEM((2, yc, LANES), F32)]
        + [pltpu.VMEM((2, zc, 1, LANES), F32)] * 3
        + [pltpu.VMEM((2, yc, LANES), F32)]
        + [pltpu.VMEM((3, 1, LANES), F32), pltpu.VMEM((ng, 3, 1, LANES), F32)]
        + [pltpu.VMEM((2, 1, LANES), F32)]
        + [pltpu.VMEM((ng, 1, LANES), F32)] * 2
        + [pltpu.VMEM((nx, 2, 8, LANES), F32)]
        + [pltpu.VMEM((nx, 8, LANES), F32)] * 2
        + [
            pltpu.SemaphoreType.DMA((10,)),
            pltpu.SemaphoreType.DMA((8,)),
            pltpu.SemaphoreType.DMA((8,)),
            pltpu.SemaphoreType.DMA((6,)),
            pltpu.SemaphoreType.DMA((6,)),
        ],
        compiler_params=pltpu.CompilerParams(
            collective_id=0, has_side_effects=True, vmem_limit_bytes=32 * 1024 * 1024
        ),
        name="sweeps",
    )(*operands)
    return pressure.reshape(rhs.shape), residual.reshape(1, 1, wells)


def solution(mesh):
    nx, ny, nz = mesh.shape["gx"], mesh.shape["gy"], mesh.shape["gz"]
    cells = P("gz", "gy", "gx")
    perfs = P("gx", ("gy", "gz"), None, None)
    owned = P("gx", ("gy", "gz"), None)

    def program(rhs, perm_x, perm_y, perm_z, storage, perf_cell, perf_well, perf_index, seg_count, bhp):
        dims = (nx, ny, nz, rhs.shape[0] // nz, rhs.shape[1] // ny, seg_count.shape[-1])
        return jax.shard_map(
            functools.partial(shards, dims),
            mesh=mesh,
            in_specs=(cells,) * 5 + (perfs,) * 3 + (owned,) * 2,
            out_specs=(cells, owned),
            check_vma=False,
        )(rhs, perm_x, perm_y, perm_z, storage, perf_cell, perf_well, perf_index, seg_count, bhp)

    return program
```

```python
import functools

import jax
import jax.numpy as jnp
from jax import lax
from jax.experimental import pallas as pl
from jax.experimental.pallas import tpu as pltpu
from jax.sharding import PartitionSpec as P

F32 = jnp.float32
BF16 = jnp.bfloat16
MESH = pl.DeviceIdType.MESH
LANES = 128
SEG = 4
BORE = 20.0


def harmonic(a, b):
    return 2.0 * a * b / (a + b)


def lane_of(shape):
    return lax.broadcasted_iota(jnp.int32, shape, len(shape) - 1)


def row_of(shape):
    return lax.broadcasted_iota(jnp.int32, shape, len(shape) - 2)


def split_lanes(x):
    high = x.astype(BF16)
    low = (x - high.astype(F32)).astype(BF16)
    return jnp.concatenate([high, low], axis=1)


def onehot_product(selector, x):
    both = jnp.dot(selector, split_lanes(x), preferred_element_type=F32)
    return both[:, :LANES] + both[:, LANES:]


def lane_spread(x, lane, shape):
    return jnp.broadcast_to(x[:, lane : lane + 1], shape)


def pack_ends(pieces):
    pair = lane_of((8, LANES)) // 2
    packed = jnp.zeros((8, LANES), F32)
    for j, piece in enumerate(pieces):
        packed = jnp.where(pair == j, pltpu.roll(piece, 2 * j + 1, 1), packed)
    return packed


def kernel(
    dims, cell_in, well_in, wgt_in, cnt_in, bhp_in, rhs_in, px_in, py_in, pz_in, st_in, p_out, res_out,
    cell_ref, well_ref, wgt_ref, cnt_ref, bhp_ref, rhs, px, py, pz, st,
    sig, left, right, ylo, yup, zface, low_m, high_m, recip, inv, low_w, high_w, src, field,
    hot_x, hot_dw, line_sel, line_sel_t, reach_first, reach_last,
    yperm, zperm, yp, ysend_perm, ysend_p, zp,
    sw_send, sw_all, row_send, rows_a, rows_b, stat_all, ports_a, ports_b,
    in_sem, halo_send, halo_recv, fan_send, fan_recv,
):
    nx, ny, nz, zc, yc, wells = dims
    ng = ny * nz
    lines = zc * yc
    pieces = lines // 8
    mx, my, mz = lax.axis_index("gx"), lax.axis_index("gy"), lax.axis_index("gz")
    mg = my * nz + mz

    def ring(offset, size):
        return min(offset, size - offset)

    group_offsets = [(dy, dz) for dy in range(ny) for dz in range(nz) if (dy, dz) != (0, 0)]
    group_offsets.sort(key=lambda o: -(ring(o[0], ny) + ring(o[1], nz)))
    group_peers = [{"gy": lax.rem(my + dy, ny), "gz": lax.rem(mz + dz, nz)} for dy, dz in group_offsets]
    x_offsets = sorted(range(1, nx), key=lambda o: -ring(o, nx))
    x_peers = [{"gx": lax.rem(mx + dx, nx)} for dx in x_offsets]

    barrier = pltpu.get_barrier_semaphore()
    for peer in group_peers + x_peers:
        pl.semaphore_signal(barrier, inc=1, device_id=peer, device_id_type=MESH)

    loads = [
        pltpu.make_async_copy(a, b, in_sem.at[i])
        for i, (a, b) in enumerate(
            (
                (py_in, py), (pz_in, pz), (px_in, px), (st_in, st), (rhs_in, rhs),
                (cell_in, cell_ref), (well_in, well_ref), (wgt_in, wgt_ref), (cnt_in, cnt_ref), (bhp_in, bhp_ref),
            )
        )
    ]
    for load in loads[5:] + loads[:5]:
        load.start()

    def fan(peers, source, target, which):
        for peer in peers:
            pltpu.make_async_remote_copy(
                src_ref=source, dst_ref=target, send_sem=fan_send.at[which], recv_sem=fan_recv.at[which],
                device_id=peer, device_id_type=MESH,
            ).start()

    def fan_wait(target, count, sems, which):
        view = target.at[pl.ds(0, count)]
        pltpu.make_async_copy(view, view, sems.at[which]).wait()

    y_next, y_prev = lax.rem(my + 1, ny), lax.rem(my + ny - 1, ny)
    z_next, z_prev = lax.rem(mz + 1, nz), lax.rem(mz + nz - 1, nz)

    def halos(y_src, y_dst, z_src, z_dst, base):
        last = pl.ds((zc - 1) * yc, yc)
        routes = (
            (y_src.at[0], y_dst.at[1], {"gy": y_prev}),
            (y_src.at[1], y_dst.at[0], {"gy": y_next}),
            (z_src.at[pl.ds(0, yc)], z_dst.at[1], {"gz": z_prev}),
            (z_src.at[last], z_dst.at[0], {"gz": z_next}),
        )
        return [
            pltpu.make_async_remote_copy(
                src_ref=a, dst_ref=b, send_sem=halo_send.at[base + i], recv_sem=halo_recv.at[base + i],
                device_id=peer, device_id_type=MESH,
            )
            for i, (a, b, peer) in enumerate(routes)
        ]

    for load in loads[5:]:
        load.wait()
    code = cell_ref[...]
    wellv = well_ref[...]
    wgtv = wgt_ref[...]
    piece = (8, LANES)
    lane8 = lane_of(piece)
    sw_row = jnp.zeros(piece, F32)
    for d in range(ng):
        mine = lane8 == lane_spread(wellv, d, piece) + d * wells
        mine = jnp.where(mine, lane_spread(wgtv, d, piece), 0.0)
        hot_dw[d * 8 : d * 8 + 8, :] = mine
        sw_row = sw_row + mine
    sw_send[0] = jnp.sum(sw_row, axis=0, keepdims=True)
    lane1 = lane_of((1, LANES))
    counts = jnp.zeros((1, LANES), F32)
    bores = jnp.zeros((1, LANES), F32)
    for w in range(wells):
        here = lane1 == mg * wells + w
        counts = jnp.where(here, cnt_ref[0, w].astype(F32), counts)
        bores = jnp.where(here, bhp_ref[0, w], bores)
    sw_send[1] = counts
    sw_send[2] = bores

    loads[0].wait()
    loads[1].wait()
    for z in range(zc):
        ysend_perm[0, z] = py[z * yc : z * yc + 1, :]
        ysend_perm[1, z] = py[z * yc + yc - 1 : z * yc + yc, :]

    pl.semaphore_wait(barrier, ng - 1 + nx - 1)
    perm_halos = halos(ysend_perm, yperm, pz, zperm, 0)
    for copy in perm_halos:
        copy.start()
    fan(group_peers, sw_send, sw_all.at[mg], 0)
    sw_all[mg] = sw_send[...]

    for d in range(ng):
        c = lane_spread(code, d, piece)
        rows = slice(d * 8, d * 8 + 8)
        hot_x[rows, :] = jnp.where(lane8 == jnp.bitwise_and(c, LANES - 1), 1.0, 0.0)
        for half in range(lines // LANES):
            hit = lane8 == jnp.right_shift(c, 7) - half * LANES
            line_sel[rows, half * LANES : half * LANES + LANES] = jnp.where(hit, 1.0, 0.0)
    line_sel_t[...] = line_sel[...].T.astype(BF16)

    loads[2].wait()
    loads[3].wait()
    lane_s = lane_of((yc, LANES))
    row_s = row_of((yc, LANES))
    for z in range(zc):
        rows = slice(z * yc, z * yc + yc)
        v = px[rows, :]
        f = jnp.where(lane_s == 0, 0.0, harmonic(pltpu.roll(v, 1, 1), v))
        left[rows, :] = f
        right[rows, :] = pltpu.roll(f, LANES - 1, 1)
        v = py[rows, :]
        f = harmonic(pltpu.roll(v, 1, 0), v)
        ylo[rows, :] = f
        if z > 0:
            zface[rows, :] = harmonic(pz[z * yc - yc : z * yc, :], pz[rows, :])
    strides = [1 << i for i in range(7)]

    def reduce_matrix(groups):
        for slices in groups:
            lo, hi, s = [jnp.concatenate([ref[rows, :] for rows in slices], axis=0) for ref in (left, right, sig)]
            lane_c = lane_of(lo.shape)

            def keep(ref, value, *at):
                start = 0
                for rows in slices:
                    size = rows.stop - rows.start
                    ref[(*at, rows, slice(None))] = value[start : start + size]
                    start += size

            for level, stride in enumerate(strides):
                r = 1.0 / (s + lo + hi)
                from_low = lane_c > stride
                from_high = lane_c < LANES - 1 - stride
                a = jnp.where(from_low, lo, 0.0)
                g = jnp.where(from_high, hi, 0.0)
                keep(low_m, a, level)
                keep(high_m, g, level)
                keep(recip, r, level)
                q = s * r
                s = s + a * pltpu.roll(q, stride, 1) + g * pltpu.roll(q, LANES - stride, 1)
                lo = jnp.where(from_low, lo * pltpu.roll(lo * r, stride, 1), lo)
                hi = jnp.where(from_high, hi * pltpu.roll(hi * r, LANES - stride, 1), hi)
            r = 1.0 / (s + lo + hi)
            first, last = lane_c == 0, lane_c == LANES - 1
            keep(inv, jnp.where(jnp.logical_or(first, last), 0.0, r))
            keep(low_w, jnp.where(first, 1.0, jnp.where(last, 0.0, lo * r)))
            keep(high_w, jnp.where(last, 1.0, jnp.where(first, 0.0, hi * r)))
            keep(sig, s)
            keep(right, hi)

    tile = 8
    inner = [[slice(z * yc + tile, z * yc + yc - tile) for z in range(1, zc - 1)]]
    edge = [slice(z * yc + o, z * yc + o + tile) for z in range(1, zc - 1) for o in (0, yc - tile)]
    cut = len(edge) // 2
    outer = [[slice(0, yc)] + edge[:cut], [slice(lines - yc, lines)] + edge[cut:]]
    for slices in inner:
        for rows in slices:
            sig[rows, :] = (
                st[rows, :] + ylo[rows, :] + ylo[rows.start + 1 : rows.stop + 1, :]
                + zface[rows, :] + zface[rows.start + yc : rows.stop + yc, :]
            )
    reduce_matrix(inner)

    for copy in perm_halos:
        copy.wait_recv()
    zface[0:yc, :] = jnp.where(mz == 0, 0.0, harmonic(zperm[0], pz[0:yc, :]))
    zface[lines : lines + yc, :] = jnp.where(mz == nz - 1, 0.0, harmonic(pz[lines - yc : lines, :], zperm[1]))
    for z in range(zc):
        rows = slice(z * yc, z * yc + yc)
        low = jnp.where(my == 0, 0.0, harmonic(yperm[0, z], py[z * yc : z * yc + 1, :]))
        top = jnp.where(my == ny - 1, 0.0, harmonic(py[z * yc + yc - 1 : z * yc + yc, :], yperm[1, z]))
        f = jnp.where(row_s == 0, low, ylo[rows, :])
        g = jnp.where(row_s == yc - 1, top, pltpu.roll(f, yc - 1, 0))
        ylo[rows, :] = f
        yup[rows, :] = g
        total = st[rows, :] + f + g + zface[rows, :] + zface[z * yc + yc : z * yc + 2 * yc, :]
        if z in (0, zc - 1):
            sig[rows, :] = total
        else:
            for o in (0, yc - tile):
                sig[z * yc + o : z * yc + o + tile, :] = total[o : o + tile]

    reduce_matrix(outer)

    def ends_of(ref):
        return pack_ends([ref[j * 8 : j * 8 + 8, :] for j in range(pieces)])

    stat_all[mx, 0] = ends_of(sig) + pltpu.roll(ends_of(px), LANES // 2, 1)
    stat_all[mx, 1] = ends_of(right)
    fan(x_peers, stat_all.at[mx], stat_all.at[mx], 1)

    def at_perforations(values):
        rows = onehot_product(line_sel[...].astype(BF16), values)
        return jnp.sum(rows * hot_x[...], axis=1, keepdims=True)

    reach_first[...] = onehot_product(line_sel_t[...], hot_dw[...] * at_perforations(low_w[...]))
    reach_last[...] = onehot_product(line_sel_t[...], hot_dw[...] * at_perforations(high_w[...]))

    pair8 = lane8 // 2
    even = lane8 % 2 == 0

    def line_ends(for_first, for_last):
        packed = jnp.zeros(piece, F32)
        for j in range(pieces):
            rows = slice(j * 8, j * 8 + 8)
            both = jnp.where(
                even,
                jnp.sum(for_last(rows), axis=1, keepdims=True),
                jnp.sum(for_first(rows), axis=1, keepdims=True),
            )
            packed = jnp.where(pair8 == j, both, packed)
        return packed

    def end_sources(values):
        return line_ends(lambda rows: low_w[rows, :] * values[rows, :], lambda rows: high_w[rows, :] * values[rows, :])

    def end_wells(seg_row):
        return line_ends(lambda rows: reach_first[rows, :] * seg_row, lambda rows: reach_last[rows, :] * seg_row)

    def send_ports(ports, packed, which):
        ports[mx] = packed + pltpu.roll(packed, LANES // 2, 1)
        fan(x_peers, ports.at[mx], ports.at[mx], which)

    def well_field(drop):
        back = jnp.sum(hot_dw[...] * drop, axis=1, keepdims=True)
        return onehot_product(line_sel_t[...], hot_x[...] * back)

    def solve_local():
        half = lines // 2
        for h in range(2):
            rows = slice(h * half, h * half + half)
            b = src[rows, :]
            for level, stride in enumerate(strides):
                t = b * recip[level, rows, :]
                b = b + low_m[level, rows, :] * pltpu.roll(t, stride, 1) + high_m[level, rows, :] * pltpu.roll(
                    t, LANES - stride, 1
                )
            src[rows, :] = b * inv[rows, :]

    def well_sums(cols):
        return jnp.sum(hot_dw[...] * cols, axis=0, keepdims=True)

    loads[4].wait()
    ends_rhs = end_sources(rhs)

    fan_wait(sw_all, ng - 1, fan_recv, 0)
    layer_all = [sum(sw_all[y * nz + g] for y in range(ny)) for g in range(nz)]
    total = sum(layer_all)
    count, bore = total[1], total[2]
    layer_sw = [layer[0] for layer in layer_all]

    def slot_of(g):
        return jnp.floor(g * count * (1.0 / nz))

    my_slot = slot_of(mz.astype(F32))
    layer_slots = [slot_of(float(g)) for g in range(nz)]
    same = [jnp.where(slot == my_slot, 1.0, 0.0) for slot in layer_slots]
    my_inv = 1.0 / (sum(m * sw for m, sw in zip(same, layer_sw)) + BORE)
    my_base = BORE * bore * my_inv
    send_ports(ports_a, ends_rhs + end_wells(my_base), 2)

    src[...] = rhs[...] + well_field(my_base)
    solve_local()
    row_own = well_sums(at_perforations(src[...]))

    fan_wait(stat_all, nx - 1, fan_recv, 1)

    def ends_at(k):
        s, c = stat_all[k, 0], stat_all[k, 1]
        return dict(
            sz=s, sf=pltpu.roll(s, LANES - 1, 1), pz=pltpu.roll(s, LANES // 2, 1),
            pf=pltpu.roll(s, LANES // 2 - 1, 1), c=pltpu.roll(c, LANES - 1, 1),
        )

    own = ends_at(mx)

    def walk(direction):
        chain = []
        for t in range(1, nx):
            k = mx + direction * t
            valid = jnp.logical_and(k >= 0, k < nx)
            chain.append((jnp.clip(k, 0, nx - 1), valid))
        blocks = [ends_at(k) for k, _ in chain]
        ground = jnp.zeros(piece, F32)
        factors = [None] * (nx - 1)
        for t in range(nx - 1, 0, -1):
            b = blocks[t - 1]
            nearer = own if t == 1 else blocks[t - 2]
            far, near, edge = ("sf", "sz", ("pz", "pf")) if direction < 0 else ("sz", "sf", ("pf", "pz"))
            face = jnp.where(chain[t - 1][1], harmonic(b[edge[0]], nearer[edge[1]]), 0.0)
            shunt = b[far] + ground
            joined = b["c"] + shunt
            inner = b[near] * joined + shunt * b["c"]
            part = face / (face * joined + inner)
            ground = inner * part
            factors[t - 1] = (part * joined, part * b["c"])
        reach = jnp.ones(piece, F32)
        weights = []
        for from_near, from_far in factors:
            weights.append((reach * from_near, reach * from_far))
            reach = weights[-1][1]
        return ground, weights, [k for k, _ in chain]

    ground_l, weights_l, index_l = walk(-1)
    ground_r, weights_r, index_r = walk(1)
    a, e, c = own["sf"] + ground_l, own["sz"] + ground_r, own["c"]
    scale = 1.0 / (a * e + (a + e) * c)
    ff, fz, zz = (e + c) * scale, c * scale, (a + c) * scale
    lower_half = lane8 < LANES // 2

    def weave(z_first, f_first, z_last, f_last):
        first = jnp.where(even, z_first, pltpu.roll(f_first, 1, 1))
        last = jnp.where(even, pltpu.roll(z_last, LANES // 2, 1), pltpu.roll(f_last, LANES // 2 + 1, 1))
        return jnp.where(lower_half, first, last)

    terms = [(mx, weave(fz, ff, zz, fz))]
    for (near_w, far_w), k in zip(weights_l, index_l):
        terms.append((k, weave(ff * near_w, ff * far_w, fz * near_w, fz * far_w)))
    for (near_w, far_w), k in zip(weights_r, index_r):
        terms.append((k, weave(fz * far_w, fz * near_w, zz * far_w, zz * near_w)))

    def end_pressures(ports):
        ends = sum(w * ports[k] for k, w in terms)
        ends = ends + pltpu.roll(ends, LANES - 1, 1)
        return [
            (lane_spread(ends, 2 * j, piece), lane_spread(ends, LANES // 2 + 2 * j, piece)) for j in range(pieces)
        ]

    def end_sums(ends):
        given = jnp.zeros(piece, F32)
        for j, (first, last) in enumerate(ends):
            rows = slice(j * 8, j * 8 + 8)
            given = given + reach_first[rows, :] * first + reach_last[rows, :] * last
        return jnp.sum(given, axis=0, keepdims=True)

    def join(ends, target):
        for j, (first, last) in enumerate(ends):
            rows = slice(j * 8, j * 8 + 8)
            target[rows, :] = src[rows, :] + low_w[rows, :] * first + high_w[rows, :] * last

    def send_row(which, row, target):
        row_send[which] = row
        fan(group_peers, row_send.at[which], target.at[mg], 3 + which)
        target[mg] = row

    fan_wait(ports_a, nx - 1, fan_recv, 2)
    ends = end_pressures(ports_a)
    send_row(0, row_own + end_sums(ends), rows_a)

    join(ends, field)
    for z in range(zc):
        ysend_p[0, z] = field[z * yc : z * yc + 1, :]
        ysend_p[1, z] = field[z * yc + yc - 1 : z * yc + yc, :]
    p_halos = halos(ysend_p, yp, field, zp, 4)
    for copy in p_halos:
        copy.start()
    cols = at_perforations(field[...])
    coef_mine = [m * my_inv for m in same]
    coef_seg = []
    for g in range(nz):
        slot_sw = sum(jnp.where(layer_slots[h] == layer_slots[g], layer_sw[h], 0.0) for h in range(nz))
        coef_seg.append(1.0 / (slot_sw + BORE))
    residual_base = bore * sum(f * sw for f, sw in zip(coef_seg, layer_sw))

    for copy in p_halos:
        copy.wait_recv()
    for z in range(zc):
        rows = slice(z * yc, z * yc + yc)
        v = field[rows, :]
        below = jnp.where(row_s == 0, yp[0, z], pltpu.roll(v, 1, 0))
        above = jnp.where(row_s == yc - 1, yp[1, z], pltpu.roll(v, yc - 1, 0))
        under = field[z * yc - yc : z * yc, :] if z > 0 else zp[0]
        over = field[z * yc + yc : z * yc + 2 * yc, :] if z < zc - 1 else zp[1]
        beside = ylo[rows, :] * below + yup[rows, :] * above
        beside = beside + zface[rows, :] * under + zface[z * yc + yc : z * yc + 2 * yc, :] * over
        src[rows, :] = rhs[rows, :] + beside
    src[...] = src[...] + well_field(my_base - cols)
    ends_base = end_sources(src)

    fan_wait(rows_a, ng - 1, fan_recv, 3)
    inflow = sum(f * sum(rows_a[y * nz + g] for y in range(ny)) for g, f in enumerate(coef_mine))
    send_ports(ports_b, ends_base + end_wells(inflow), 5)
    src[...] = src[...] + well_field(inflow)
    solve_local()
    row_own = well_sums(at_perforations(src[...]))
    fan_wait(ports_b, nx - 1, fan_recv, 5)
    ends = end_pressures(ports_b)
    send_row(1, row_own + end_sums(ends), rows_b)
    join(ends, p_out)
    fan_wait(rows_b, ng - 1, fan_recv, 4)
    res = sum(f * sum(rows_b[y * nz + g] for y in range(ny)) for g, f in enumerate(coef_seg)) - residual_base
    res_out[...] = pltpu.roll(res, lax.rem(LANES - mg * wells, LANES), 1)[:, :wells]

    for copy in perm_halos + p_halos:
        copy.wait_send()
    fan_wait(sw_all, ng - 1, fan_send, 0)
    fan_wait(stat_all, nx - 1, fan_send, 1)
    fan_wait(ports_a, nx - 1, fan_send, 2)
    fan_wait(rows_a, ng - 1, fan_send, 3)
    fan_wait(rows_b, ng - 1, fan_send, 4)
    fan_wait(ports_b, nx - 1, fan_send, 5)


def shards(dims, rhs, perm_x, perm_y, perm_z, storage, perf_cell, perf_well, perf_index, seg_count, bhp):
    nx, ny, nz, zc, yc, wells = dims
    ng = ny * nz
    lines = zc * yc
    perfs = ng * 8
    plane = (lines, LANES)
    flat = [a.reshape(plane) for a in (rhs, perm_x, perm_y, perm_z, storage)]
    slots = [a[0, 0].T for a in (perf_cell, perf_well, perf_index)]
    operands = [pltpu.with_memory_space_constraint(a, pltpu.HBM) for a in (*slots, seg_count[0], bhp[0], *flat)]
    vmem = pl.BlockSpec(memory_space=pltpu.VMEM)
    hbm = pl.BlockSpec(memory_space=pltpu.HBM)
    whole = pltpu.VMEM(plane, F32)
    perf_plane = pltpu.VMEM((perfs, LANES), F32)
    pressure, residual = pl.pallas_call(
        functools.partial(kernel, dims),
        out_shape=(pltpu.VMEM(plane, F32), pltpu.VMEM((1, wells), F32)),
        in_specs=[hbm] * 10,
        out_specs=(vmem, vmem),
        scratch_shapes=[pltpu.VMEM((8, ng), jnp.int32)] * 2
        + [pltpu.VMEM((8, ng), F32), pltpu.SMEM((1, wells), jnp.int32), pltpu.SMEM((1, wells), F32)]
        + [whole] * 5
        + [whole] * 5
        + [pltpu.VMEM((lines + yc, LANES), F32)]
        + [pltpu.VMEM((7, lines, LANES), F32)] * 3
        + [whole] * 5
        + [perf_plane] * 2
        + [pltpu.VMEM((perfs, lines), F32), pltpu.VMEM((lines, perfs), BF16)]
        + [whole] * 2
        + [pltpu.VMEM((2, zc, 1, LANES), F32), pltpu.VMEM((2, yc, LANES), F32)]
        + [pltpu.VMEM((2, zc, 1, LANES), F32)] * 3
        + [pltpu.VMEM((2, yc, LANES), F32)]
        + [pltpu.VMEM((3, 1, LANES), F32), pltpu.VMEM((ng, 3, 1, LANES), F32)]
        + [pltpu.VMEM((2, 1, LANES), F32)]
        + [pltpu.VMEM((ng, 1, LANES), F32)] * 2
        + [pltpu.VMEM((nx, 2, 8, LANES), F32)]
        + [pltpu.VMEM((nx, 8, LANES), F32)] * 2
        + [
            pltpu.SemaphoreType.DMA((10,)),
            pltpu.SemaphoreType.DMA((8,)),
            pltpu.SemaphoreType.DMA((8,)),
            pltpu.SemaphoreType.DMA((6,)),
            pltpu.SemaphoreType.DMA((6,)),
        ],
        compiler_params=pltpu.CompilerParams(
            collective_id=0, has_side_effects=True, vmem_limit_bytes=32 * 1024 * 1024
        ),
        name="sweeps",
    )(*operands)
    return pressure.reshape(rhs.shape), residual.reshape(1, 1, wells)


def solution(mesh):
    nx, ny, nz = mesh.shape["gx"], mesh.shape["gy"], mesh.shape["gz"]
    cells = P("gz", "gy", "gx")
    perfs = P("gx", ("gy", "gz"), None, None)
    owned = P("gx", ("gy", "gz"), None)

    def program(rhs, perm_x, perm_y, perm_z, storage, perf_cell, perf_well, perf_index, seg_count, bhp):
        dims = (nx, ny, nz, rhs.shape[0] // nz, rhs.shape[1] // ny, seg_count.shape[-1])
        return jax.shard_map(
            functools.partial(shards, dims),
            mesh=mesh,
            in_specs=(cells,) * 5 + (perfs,) * 3 + (owned,) * 2,
            out_specs=(cells, owned),
            check_vma=False,
        )(rhs, perm_x, perm_y, perm_z, storage, perf_cell, perf_well, perf_index, seg_count, bhp)

    return program
```

```python
import functools

import jax
import jax.numpy as jnp
from jax import lax
from jax.experimental import pallas as pl
from jax.experimental.pallas import tpu as pltpu
from jax.sharding import PartitionSpec as P

F32 = jnp.float32
BF16 = jnp.bfloat16
MESH = pl.DeviceIdType.MESH
LANES = 128
SEG = 4
BORE = 20.0


def harmonic(a, b):
    return 2.0 * a * b / (a + b)


def lane_of(shape):
    return lax.broadcasted_iota(jnp.int32, shape, len(shape) - 1)


def row_of(shape):
    return lax.broadcasted_iota(jnp.int32, shape, len(shape) - 2)


def split_lanes(x):
    high = x.astype(BF16)
    low = (x - high.astype(F32)).astype(BF16)
    return jnp.concatenate([high, low], axis=1)


def onehot_product(selector, x):
    both = jnp.dot(selector, split_lanes(x), preferred_element_type=F32)
    return both[:, :LANES] + both[:, LANES:]


def lane_spread(x, lane, shape):
    return jnp.broadcast_to(x[:, lane : lane + 1], shape)


def pack_ends(pieces):
    pair = lane_of((8, LANES)) // 2
    packed = jnp.zeros((8, LANES), F32)
    for j, piece in enumerate(pieces):
        packed = jnp.where(pair == j, pltpu.roll(piece, 2 * j + 1, 1), packed)
    return packed


def kernel(
    dims, cell_in, well_in, wgt_in, cnt_in, bhp_in, rhs_in, px_in, py_in, pz_in, st_in, p_out, res_out,
    cell_ref, well_ref, wgt_ref, cnt_ref, bhp_ref, rhs, px, py, pz, st,
    sig, left, right, ylo, yup, zface, low_m, high_m, recip, inv, low_w, high_w, src, field,
    hot_x, hot_dw, line_sel, line_sel_t, reach_first, reach_last,
    yperm, zperm, yp, ysend_perm, ysend_p, zp,
    sw_send, sw_all, row_send, rows_a, rows_b, stat_all, ports_a, ports_b,
    in_sem, halo_send, halo_recv, fan_send, fan_recv,
):
    nx, ny, nz, zc, yc, wells = dims
    ng = ny * nz
    lines = zc * yc
    pieces = lines // 8
    mx, my, mz = lax.axis_index("gx"), lax.axis_index("gy"), lax.axis_index("gz")
    mg = my * nz + mz

    def ring(offset, size):
        return min(offset, size - offset)

    group_offsets = [(dy, dz) for dy in range(ny) for dz in range(nz) if (dy, dz) != (0, 0)]
    group_offsets.sort(key=lambda o: -(ring(o[0], ny) + ring(o[1], nz)))
    group_peers = [{"gy": lax.rem(my + dy, ny), "gz": lax.rem(mz + dz, nz)} for dy, dz in group_offsets]
    x_offsets = sorted(range(1, nx), key=lambda o: -ring(o, nx))
    x_peers = [{"gx": lax.rem(mx + dx, nx)} for dx in x_offsets]

    barrier = pltpu.get_barrier_semaphore()
    for peer in group_peers + x_peers:
        pl.semaphore_signal(barrier, inc=1, device_id=peer, device_id_type=MESH)

    loads = [
        pltpu.make_async_copy(a, b, in_sem.at[i])
        for i, (a, b) in enumerate(
            (
                (py_in, py), (pz_in, pz), (px_in, px), (st_in, st), (rhs_in, rhs),
                (cell_in, cell_ref), (well_in, well_ref), (wgt_in, wgt_ref), (cnt_in, cnt_ref), (bhp_in, bhp_ref),
            )
        )
    ]
    for load in loads[5:] + loads[:5]:
        load.start()

    def fan(peers, source, target, which):
        for peer in peers:
            pltpu.make_async_remote_copy(
                src_ref=source, dst_ref=target, send_sem=fan_send.at[which], recv_sem=fan_recv.at[which],
                device_id=peer, device_id_type=MESH,
            ).start()

    def fan_wait(target, count, sems, which):
        view = target.at[pl.ds(0, count)]
        pltpu.make_async_copy(view, view, sems.at[which]).wait()

    y_next, y_prev = lax.rem(my + 1, ny), lax.rem(my + ny - 1, ny)
    z_next, z_prev = lax.rem(mz + 1, nz), lax.rem(mz + nz - 1, nz)

    def halos(y_src, y_dst, z_src, z_dst, base):
        last = pl.ds((zc - 1) * yc, yc)
        routes = (
            (y_src.at[0], y_dst.at[1], {"gy": y_prev}),
            (y_src.at[1], y_dst.at[0], {"gy": y_next}),
            (z_src.at[pl.ds(0, yc)], z_dst.at[1], {"gz": z_prev}),
            (z_src.at[last], z_dst.at[0], {"gz": z_next}),
        )
        return [
            pltpu.make_async_remote_copy(
                src_ref=a, dst_ref=b, send_sem=halo_send.at[base + i], recv_sem=halo_recv.at[base + i],
                device_id=peer, device_id_type=MESH,
            )
            for i, (a, b, peer) in enumerate(routes)
        ]

    for load in loads[5:]:
        load.wait()
    code = cell_ref[...]
    wellv = well_ref[...]
    wgtv = wgt_ref[...]
    piece = (8, LANES)
    lane8 = lane_of(piece)
    sw_row = jnp.zeros(piece, F32)
    for d in range(ng):
        mine = lane8 == lane_spread(wellv, d, piece) + d * wells
        mine = jnp.where(mine, lane_spread(wgtv, d, piece), 0.0)
        hot_dw[d * 8 : d * 8 + 8, :] = mine
        sw_row = sw_row + mine
    sw_send[0] = jnp.sum(sw_row, axis=0, keepdims=True)
    lane1 = lane_of((1, LANES))
    counts = jnp.zeros((1, LANES), F32)
    bores = jnp.zeros((1, LANES), F32)
    for w in range(wells):
        here = lane1 == mg * wells + w
        counts = jnp.where(here, cnt_ref[0, w].astype(F32), counts)
        bores = jnp.where(here, bhp_ref[0, w], bores)
    sw_send[1] = counts
    sw_send[2] = bores

    loads[0].wait()
    loads[1].wait()
    for z in range(zc):
        ysend_perm[0, z] = py[z * yc : z * yc + 1, :]
        ysend_perm[1, z] = py[z * yc + yc - 1 : z * yc + yc, :]

    pl.semaphore_wait(barrier, ng - 1 + nx - 1)
    perm_halos = halos(ysend_perm, yperm, pz, zperm, 0)
    for copy in perm_halos:
        copy.start()
    fan(group_peers, sw_send, sw_all.at[mg], 0)
    sw_all[mg] = sw_send[...]

    for d in range(ng):
        c = lane_spread(code, d, piece)
        rows = slice(d * 8, d * 8 + 8)
        hot_x[rows, :] = jnp.where(lane8 == jnp.bitwise_and(c, LANES - 1), 1.0, 0.0)
        for half in range(lines // LANES):
            hit = lane8 == jnp.right_shift(c, 7) - half * LANES
            line_sel[rows, half * LANES : half * LANES + LANES] = jnp.where(hit, 1.0, 0.0)
    line_sel_t[...] = line_sel[...].T.astype(BF16)

    loads[2].wait()
    loads[3].wait()
    lane_s = lane_of((yc, LANES))
    row_s = row_of((yc, LANES))
    for z in range(zc):
        rows = slice(z * yc, z * yc + yc)
        v = px[rows, :]
        f = jnp.where(lane_s == 0, 0.0, harmonic(pltpu.roll(v, 1, 1), v))
        left[rows, :] = f
        right[rows, :] = pltpu.roll(f, LANES - 1, 1)
        v = py[rows, :]
        f = harmonic(pltpu.roll(v, 1, 0), v)
        ylo[rows, :] = f
        if z > 0:
            zface[rows, :] = harmonic(pz[z * yc - yc : z * yc, :], pz[rows, :])
    strides = [1 << i for i in range(7)]

    def reduce_matrix(groups):
        for slices in groups:
            lo, hi, s = [jnp.concatenate([ref[rows, :] for rows in slices], axis=0) for ref in (left, right, sig)]
            lane_c = lane_of(lo.shape)

            def keep(ref, value, *at):
                start = 0
                for rows in slices:
                    size = rows.stop - rows.start
                    ref[(*at, rows, slice(None))] = value[start : start + size]
                    start += size

            for level, stride in enumerate(strides):
                r = 1.0 / (s + lo + hi)
                from_low = lane_c > stride
                from_high = lane_c < LANES - 1 - stride
                a = jnp.where(from_low, lo, 0.0)
                g = jnp.where(from_high, hi, 0.0)
                keep(low_m, a, level)
                keep(high_m, g, level)
                keep(recip, r, level)
                q = s * r
                s = s + a * pltpu.roll(q, stride, 1) + g * pltpu.roll(q, LANES - stride, 1)
                lo = jnp.where(from_low, lo * pltpu.roll(lo * r, stride, 1), lo)
                hi = jnp.where(from_high, hi * pltpu.roll(hi * r, LANES - stride, 1), hi)
            r = 1.0 / (s + lo + hi)
            first, last = lane_c == 0, lane_c == LANES - 1
            keep(inv, jnp.where(jnp.logical_or(first, last), 0.0, r))
            keep(low_w, jnp.where(first, 1.0, jnp.where(last, 0.0, lo * r)))
            keep(high_w, jnp.where(last, 1.0, jnp.where(first, 0.0, hi * r)))
            keep(sig, s)
            keep(right, hi)

    tile = 8
    inner = [[slice(z * yc + tile, z * yc + yc - tile) for z in range(1, zc - 1)]]
    edge = [slice(z * yc + o, z * yc + o + tile) for z in range(1, zc - 1) for o in (0, yc - tile)]
    cut = len(edge) // 2
    outer = [[slice(0, yc)] + edge[:cut], [slice(lines - yc, lines)] + edge[cut:]]
    for slices in inner:
        for rows in slices:
            sig[rows, :] = (
                st[rows, :] + ylo[rows, :] + ylo[rows.start + 1 : rows.stop + 1, :]
                + zface[rows, :] + zface[rows.start + yc : rows.stop + yc, :]
            )
    reduce_matrix(inner)

    for copy in perm_halos:
        copy.wait_recv()
    zface[0:yc, :] = jnp.where(mz == 0, 0.0, harmonic(zperm[0], pz[0:yc, :]))
    zface[lines : lines + yc, :] = jnp.where(mz == nz - 1, 0.0, harmonic(pz[lines - yc : lines, :], zperm[1]))
    for z in range(zc):
        rows = slice(z * yc, z * yc + yc)
        low = jnp.where(my == 0, 0.0, harmonic(yperm[0, z], py[z * yc : z * yc + 1, :]))
        top = jnp.where(my == ny - 1, 0.0, harmonic(py[z * yc + yc - 1 : z * yc + yc, :], yperm[1, z]))
        f = jnp.where(row_s == 0, low, ylo[rows, :])
        g = jnp.where(row_s == yc - 1, top, pltpu.roll(f, yc - 1, 0))
        ylo[rows, :] = f
        yup[rows, :] = g
        total = st[rows, :] + f + g + zface[rows, :] + zface[z * yc + yc : z * yc + 2 * yc, :]
        if z in (0, zc - 1):
            sig[rows, :] = total
        else:
            for o in (0, yc - tile):
                sig[z * yc + o : z * yc + o + tile, :] = total[o : o + tile]

    reduce_matrix(outer)

    def ends_of(ref):
        return pack_ends([ref[j * 8 : j * 8 + 8, :] for j in range(pieces)])

    stat_all[mx, 0] = ends_of(sig) + pltpu.roll(ends_of(px), LANES // 2, 1)
    stat_all[mx, 1] = ends_of(right)
    fan(x_peers, stat_all.at[mx], stat_all.at[mx], 1)

    def at_perforations(values):
        rows = onehot_product(line_sel[...].astype(BF16), values)
        return jnp.sum(rows * hot_x[...], axis=1, keepdims=True)

    reach_first[...] = onehot_product(line_sel_t[...], hot_dw[...] * at_perforations(low_w[...]))
    reach_last[...] = onehot_product(line_sel_t[...], hot_dw[...] * at_perforations(high_w[...]))

    pair8 = lane8 // 2
    even = lane8 % 2 == 0

    def line_ends(for_first, for_last):
        packed = jnp.zeros(piece, F32)
        for j in range(pieces):
            rows = slice(j * 8, j * 8 + 8)
            both = jnp.where(
                even,
                jnp.sum(for_last(rows), axis=1, keepdims=True),
                jnp.sum(for_first(rows), axis=1, keepdims=True),
            )
            packed = jnp.where(pair8 == j, both, packed)
        return packed

    def end_sources(values):
        return line_ends(lambda rows: low_w[rows, :] * values[rows, :], lambda rows: high_w[rows, :] * values[rows, :])

    def end_wells(seg_row):
        return line_ends(lambda rows: reach_first[rows, :] * seg_row, lambda rows: reach_last[rows, :] * seg_row)

    def send_ports(ports, packed, which):
        ports[mx] = packed + pltpu.roll(packed, LANES // 2, 1)
        fan(x_peers, ports.at[mx], ports.at[mx], which)

    def well_field(drop):
        back = jnp.sum(hot_dw[...] * drop, axis=1, keepdims=True)
        return onehot_product(line_sel_t[...], hot_x[...] * back)

    def solve_local():
        size = 128

        def part(i, carry):
            rows = pl.ds(pl.multiple_of(i * size, size), size)
            b = src[rows, :]
            for level, stride in enumerate(strides):
                t = b * recip[level, rows, :]
                b = b + low_m[level, rows, :] * pltpu.roll(t, stride, 1) + high_m[level, rows, :] * pltpu.roll(
                    t, LANES - stride, 1
                )
            src[rows, :] = b * inv[rows, :]
            return carry

        lax.fori_loop(0, lines // size, part, 0)

    def well_sums(cols):
        return jnp.sum(hot_dw[...] * cols, axis=0, keepdims=True)

    loads[4].wait()
    ends_rhs = end_sources(rhs)

    fan_wait(sw_all, ng - 1, fan_recv, 0)
    layer_all = [sum(sw_all[y * nz + g] for y in range(ny)) for g in range(nz)]
    total = sum(layer_all)
    count, bore = total[1], total[2]
    layer_sw = [layer[0] for layer in layer_all]

    def slot_of(g):
        return jnp.floor(g * count * (1.0 / nz))

    my_slot = slot_of(mz.astype(F32))
    layer_slots = [slot_of(float(g)) for g in range(nz)]
    same = [jnp.where(slot == my_slot, 1.0, 0.0) for slot in layer_slots]
    my_inv = 1.0 / (sum(m * sw for m, sw in zip(same, layer_sw)) + BORE)
    my_base = BORE * bore * my_inv
    send_ports(ports_a, ends_rhs + end_wells(my_base), 2)

    src[...] = rhs[...] + well_field(my_base)
    solve_local()
    row_own = well_sums(at_perforations(src[...]))

    fan_wait(stat_all, nx - 1, fan_recv, 1)

    def ends_at(k):
        s, c = stat_all[k, 0], stat_all[k, 1]
        return dict(
            sz=s, sf=pltpu.roll(s, LANES - 1, 1), pz=pltpu.roll(s, LANES // 2, 1),
            pf=pltpu.roll(s, LANES // 2 - 1, 1), c=pltpu.roll(c, LANES - 1, 1),
        )

    own = ends_at(mx)

    def walk(direction):
        chain = []
        for t in range(1, nx):
            k = mx + direction * t
            valid = jnp.logical_and(k >= 0, k < nx)
            chain.append((jnp.clip(k, 0, nx - 1), valid))
        blocks = [ends_at(k) for k, _ in chain]
        ground = jnp.zeros(piece, F32)
        factors = [None] * (nx - 1)
        for t in range(nx - 1, 0, -1):
            b = blocks[t - 1]
            nearer = own if t == 1 else blocks[t - 2]
            far, near, edge = ("sf", "sz", ("pz", "pf")) if direction < 0 else ("sz", "sf", ("pf", "pz"))
            face = jnp.where(chain[t - 1][1], harmonic(b[edge[0]], nearer[edge[1]]), 0.0)
            shunt = b[far] + ground
            joined = b["c"] + shunt
            inner = b[near] * joined + shunt * b["c"]
            part = face / (face * joined + inner)
            ground = inner * part
            factors[t - 1] = (part * joined, part * b["c"])
        reach = jnp.ones(piece, F32)
        weights = []
        for from_near, from_far in factors:
            weights.append((reach * from_near, reach * from_far))
            reach = weights[-1][1]
        return ground, weights, [k for k, _ in chain]

    ground_l, weights_l, index_l = walk(-1)
    ground_r, weights_r, index_r = walk(1)
    a, e, c = own["sf"] + ground_l, own["sz"] + ground_r, own["c"]
    scale = 1.0 / (a * e + (a + e) * c)
    ff, fz, zz = (e + c) * scale, c * scale, (a + c) * scale
    lower_half = lane8 < LANES // 2

    def weave(z_first, f_first, z_last, f_last):
        first = jnp.where(even, z_first, pltpu.roll(f_first, 1, 1))
        last = jnp.where(even, pltpu.roll(z_last, LANES // 2, 1), pltpu.roll(f_last, LANES // 2 + 1, 1))
        return jnp.where(lower_half, first, last)

    terms = [(mx, weave(fz, ff, zz, fz))]
    for (near_w, far_w), k in zip(weights_l, index_l):
        terms.append((k, weave(ff * near_w, ff * far_w, fz * near_w, fz * far_w)))
    for (near_w, far_w), k in zip(weights_r, index_r):
        terms.append((k, weave(fz * far_w, fz * near_w, zz * far_w, zz * near_w)))

    def end_pressures(ports):
        ends = sum(w * ports[k] for k, w in terms)
        ends = ends + pltpu.roll(ends, LANES - 1, 1)
        return [
            (lane_spread(ends, 2 * j, piece), lane_spread(ends, LANES // 2 + 2 * j, piece)) for j in range(pieces)
        ]

    def end_sums(ends):
        given = jnp.zeros(piece, F32)
        for j, (first, last) in enumerate(ends):
            rows = slice(j * 8, j * 8 + 8)
            given = given + reach_first[rows, :] * first + reach_last[rows, :] * last
        return jnp.sum(given, axis=0, keepdims=True)

    def join(ends, target):
        for j, (first, last) in enumerate(ends):
            rows = slice(j * 8, j * 8 + 8)
            target[rows, :] = src[rows, :] + low_w[rows, :] * first + high_w[rows, :] * last

    def send_row(which, row, target):
        row_send[which] = row
        fan(group_peers, row_send.at[which], target.at[mg], 3 + which)
        target[mg] = row

    fan_wait(ports_a, nx - 1, fan_recv, 2)
    ends = end_pressures(ports_a)
    send_row(0, row_own + end_sums(ends), rows_a)

    join(ends, field)
    for z in range(zc):
        ysend_p[0, z] = field[z * yc : z * yc + 1, :]
        ysend_p[1, z] = field[z * yc + yc - 1 : z * yc + yc, :]
    p_halos = halos(ysend_p, yp, field, zp, 4)
    for copy in p_halos:
        copy.start()
    cols = at_perforations(field[...])
    coef_mine = [m * my_inv for m in same]
    coef_seg = []
    for g in range(nz):
        slot_sw = sum(jnp.where(layer_slots[h] == layer_slots[g], layer_sw[h], 0.0) for h in range(nz))
        coef_seg.append(1.0 / (slot_sw + BORE))
    residual_base = bore * sum(f * sw for f, sw in zip(coef_seg, layer_sw))

    for copy in p_halos:
        copy.wait_recv()
    for z in range(zc):
        rows = slice(z * yc, z * yc + yc)
        v = field[rows, :]
        below = jnp.where(row_s == 0, yp[0, z], pltpu.roll(v, 1, 0))
        above = jnp.where(row_s == yc - 1, yp[1, z], pltpu.roll(v, yc - 1, 0))
        under = field[z * yc - yc : z * yc, :] if z > 0 else zp[0]
        over = field[z * yc + yc : z * yc + 2 * yc, :] if z < zc - 1 else zp[1]
        beside = ylo[rows, :] * below + yup[rows, :] * above
        beside = beside + zface[rows, :] * under + zface[z * yc + yc : z * yc + 2 * yc, :] * over
        src[rows, :] = rhs[rows, :] + beside
    src[...] = src[...] + well_field(my_base - cols)
    ends_base = end_sources(src)

    fan_wait(rows_a, ng - 1, fan_recv, 3)
    inflow = sum(f * sum(rows_a[y * nz + g] for y in range(ny)) for g, f in enumerate(coef_mine))
    send_ports(ports_b, ends_base + end_wells(inflow), 5)
    src[...] = src[...] + well_field(inflow)
    solve_local()
    row_own = well_sums(at_perforations(src[...]))
    fan_wait(ports_b, nx - 1, fan_recv, 5)
    ends = end_pressures(ports_b)
    send_row(1, row_own + end_sums(ends), rows_b)
    join(ends, p_out)
    fan_wait(rows_b, ng - 1, fan_recv, 4)
    res = sum(f * sum(rows_b[y * nz + g] for y in range(ny)) for g, f in enumerate(coef_seg)) - residual_base
    res_out[...] = pltpu.roll(res, lax.rem(LANES - mg * wells, LANES), 1)[:, :wells]

    for copy in perm_halos + p_halos:
        copy.wait_send()
    fan_wait(sw_all, ng - 1, fan_send, 0)
    fan_wait(stat_all, nx - 1, fan_send, 1)
    fan_wait(ports_a, nx - 1, fan_send, 2)
    fan_wait(rows_a, ng - 1, fan_send, 3)
    fan_wait(rows_b, ng - 1, fan_send, 4)
    fan_wait(ports_b, nx - 1, fan_send, 5)


def shards(dims, rhs, perm_x, perm_y, perm_z, storage, perf_cell, perf_well, perf_index, seg_count, bhp):
    nx, ny, nz, zc, yc, wells = dims
    ng = ny * nz
    lines = zc * yc
    perfs = ng * 8
    plane = (lines, LANES)
    flat = [a.reshape(plane) for a in (rhs, perm_x, perm_y, perm_z, storage)]
    slots = [a[0, 0].T for a in (perf_cell, perf_well, perf_index)]
    operands = [pltpu.with_memory_space_constraint(a, pltpu.HBM) for a in (*slots, seg_count[0], bhp[0], *flat)]
    vmem = pl.BlockSpec(memory_space=pltpu.VMEM)
    hbm = pl.BlockSpec(memory_space=pltpu.HBM)
    whole = pltpu.VMEM(plane, F32)
    perf_plane = pltpu.VMEM((perfs, LANES), F32)
    pressure, residual = pl.pallas_call(
        functools.partial(kernel, dims),
        out_shape=(pltpu.VMEM(plane, F32), pltpu.VMEM((1, wells), F32)),
        in_specs=[hbm] * 10,
        out_specs=(vmem, vmem),
        scratch_shapes=[pltpu.VMEM((8, ng), jnp.int32)] * 2
        + [pltpu.VMEM((8, ng), F32), pltpu.SMEM((1, wells), jnp.int32), pltpu.SMEM((1, wells), F32)]
        + [whole] * 5
        + [whole] * 5
        + [pltpu.VMEM((lines + yc, LANES), F32)]
        + [pltpu.VMEM((7, lines, LANES), F32)] * 3
        + [whole] * 5
        + [perf_plane] * 2
        + [pltpu.VMEM((perfs, lines), F32), pltpu.VMEM((lines, perfs), BF16)]
        + [whole] * 2
        + [pltpu.VMEM((2, zc, 1, LANES), F32), pltpu.VMEM((2, yc, LANES), F32)]
        + [pltpu.VMEM((2, zc, 1, LANES), F32)] * 3
        + [pltpu.VMEM((2, yc, LANES), F32)]
        + [pltpu.VMEM((3, 1, LANES), F32), pltpu.VMEM((ng, 3, 1, LANES), F32)]
        + [pltpu.VMEM((2, 1, LANES), F32)]
        + [pltpu.VMEM((ng, 1, LANES), F32)] * 2
        + [pltpu.VMEM((nx, 2, 8, LANES), F32)]
        + [pltpu.VMEM((nx, 8, LANES), F32)] * 2
        + [
            pltpu.SemaphoreType.DMA((10,)),
            pltpu.SemaphoreType.DMA((8,)),
            pltpu.SemaphoreType.DMA((8,)),
            pltpu.SemaphoreType.DMA((6,)),
            pltpu.SemaphoreType.DMA((6,)),
        ],
        compiler_params=pltpu.CompilerParams(
            collective_id=0, has_side_effects=True, vmem_limit_bytes=32 * 1024 * 1024
        ),
        name="sweeps",
    )(*operands)
    return pressure.reshape(rhs.shape), residual.reshape(1, 1, wells)


def solution(mesh):
    nx, ny, nz = mesh.shape["gx"], mesh.shape["gy"], mesh.shape["gz"]
    cells = P("gz", "gy", "gx")
    perfs = P("gx", ("gy", "gz"), None, None)
    owned = P("gx", ("gy", "gz"), None)

    def program(rhs, perm_x, perm_y, perm_z, storage, perf_cell, perf_well, perf_index, seg_count, bhp):
        dims = (nx, ny, nz, rhs.shape[0] // nz, rhs.shape[1] // ny, seg_count.shape[-1])
        return jax.shard_map(
            functools.partial(shards, dims),
            mesh=mesh,
            in_specs=(cells,) * 5 + (perfs,) * 3 + (owned,) * 2,
            out_specs=(cells, owned),
            check_vma=False,
        )(rhs, perm_x, perm_y, perm_z, storage, perf_cell, perf_well, perf_index, seg_count, bhp)

    return program
```

```python
import functools

import jax
import jax.numpy as jnp
from jax import lax
from jax.experimental import pallas as pl
from jax.experimental.pallas import tpu as pltpu
from jax.sharding import PartitionSpec as P

F32 = jnp.float32
BF16 = jnp.bfloat16
MESH = pl.DeviceIdType.MESH
LANES = 128
SEG = 4
BORE = 20.0


def harmonic(a, b):
    return 2.0 * a * b / (a + b)


def lane_of(shape):
    return lax.broadcasted_iota(jnp.int32, shape, len(shape) - 1)


def row_of(shape):
    return lax.broadcasted_iota(jnp.int32, shape, len(shape) - 2)


def split_lanes(x):
    high = x.astype(BF16)
    low = (x - high.astype(F32)).astype(BF16)
    return jnp.concatenate([high, low], axis=1)


def onehot_product(selector, x):
    both = jnp.dot(selector, split_lanes(x), preferred_element_type=F32)
    return both[:, :LANES] + both[:, LANES:]


def lane_spread(x, lane, shape):
    return jnp.broadcast_to(x[:, lane : lane + 1], shape)


def tree_sum(values):
    values = list(values)
    while len(values) > 1:
        pairs = [a + b for a, b in zip(values[::2], values[1::2])]
        values = pairs + values[len(pairs) * 2 :]
    return values[0]


def pack_ends(pieces):
    pair = lane_of((8, LANES)) // 2
    packed = jnp.zeros((8, LANES), F32)
    for j, piece in enumerate(pieces):
        packed = jnp.where(pair == j, pltpu.roll(piece, 2 * j + 1, 1), packed)
    return packed


def kernel(
    dims, cell_in, well_in, wgt_in, cnt_in, bhp_in, rhs_in, px_in, py_in, pz_in, st_in, p_out, res_out,
    cell_ref, well_ref, wgt_ref, cnt_ref, bhp_ref, rhs, px, py, pz, st,
    sig, left, right, ylo, yup, zface, low_m, high_m, recip, inv, low_w, high_w, src, field,
    hot_x, hot_dw, line_sel, line_sel_b, line_sel_t, reach_first, reach_last,
    yperm, zperm, yp, ysend_perm, ysend_p, zp,
    sw_send, sw_all, row_send, rows_a, rows_b, stat_all, ports_a, ports_b,
    in_sem, halo_send, halo_recv, fan_send, fan_recv,
):
    nx, ny, nz, zc, yc, wells = dims
    ng = ny * nz
    lines = zc * yc
    pieces = lines // 8
    mx, my, mz = lax.axis_index("gx"), lax.axis_index("gy"), lax.axis_index("gz")
    mg = my * nz + mz

    def ring(offset, size):
        return min(offset, size - offset)

    group_offsets = [(dy, dz) for dy in range(ny) for dz in range(nz) if (dy, dz) != (0, 0)]
    group_offsets.sort(key=lambda o: -(ring(o[0], ny) + ring(o[1], nz)))
    group_peers = [{"gy": lax.rem(my + dy, ny), "gz": lax.rem(mz + dz, nz)} for dy, dz in group_offsets]
    x_offsets = sorted(range(1, nx), key=lambda o: -ring(o, nx))
    x_peers = [{"gx": lax.rem(mx + dx, nx)} for dx in x_offsets]

    barrier = pltpu.get_barrier_semaphore()
    for peer in group_peers + x_peers:
        pl.semaphore_signal(barrier, inc=1, device_id=peer, device_id_type=MESH)

    loads = [
        pltpu.make_async_copy(a, b, in_sem.at[i])
        for i, (a, b) in enumerate(
            (
                (py_in, py), (pz_in, pz), (px_in, px), (st_in, st), (rhs_in, rhs),
                (cell_in, cell_ref), (well_in, well_ref), (wgt_in, wgt_ref), (cnt_in, cnt_ref), (bhp_in, bhp_ref),
            )
        )
    ]
    for load in loads[5:] + loads[:5]:
        load.start()

    def fan(peers, source, target, which):
        for peer in peers:
            pltpu.make_async_remote_copy(
                src_ref=source, dst_ref=target, send_sem=fan_send.at[which], recv_sem=fan_recv.at[which],
                device_id=peer, device_id_type=MESH,
            ).start()

    def fan_wait(target, count, sems, which):
        view = target.at[pl.ds(0, count)]
        pltpu.make_async_copy(view, view, sems.at[which]).wait()

    y_next, y_prev = lax.rem(my + 1, ny), lax.rem(my + ny - 1, ny)
    z_next, z_prev = lax.rem(mz + 1, nz), lax.rem(mz + nz - 1, nz)

    def halos(y_src, y_dst, z_src, z_dst, base):
        last = pl.ds((zc - 1) * yc, yc)
        routes = (
            (y_src.at[0], y_dst.at[1], {"gy": y_prev}),
            (y_src.at[1], y_dst.at[0], {"gy": y_next}),
            (z_src.at[pl.ds(0, yc)], z_dst.at[1], {"gz": z_prev}),
            (z_src.at[last], z_dst.at[0], {"gz": z_next}),
        )
        return [
            pltpu.make_async_remote_copy(
                src_ref=a, dst_ref=b, send_sem=halo_send.at[base + i], recv_sem=halo_recv.at[base + i],
                device_id=peer, device_id_type=MESH,
            )
            for i, (a, b, peer) in enumerate(routes)
        ]

    for load in loads[5:]:
        load.wait()
    code = cell_ref[...]
    wellv = well_ref[...]
    wgtv = wgt_ref[...]
    piece = (8, LANES)
    lane8 = lane_of(piece)
    sw_row = jnp.zeros(piece, F32)
    for d in range(ng):
        mine = lane8 == lane_spread(wellv, d, piece) + d * wells
        mine = jnp.where(mine, lane_spread(wgtv, d, piece), 0.0)
        hot_dw[d * 8 : d * 8 + 8, :] = mine
        sw_row = sw_row + mine
    sw_send[0] = jnp.sum(sw_row, axis=0, keepdims=True)
    lane1 = lane_of((1, LANES))
    counts = jnp.zeros((1, LANES), F32)
    bores = jnp.zeros((1, LANES), F32)
    for w in range(wells):
        here = lane1 == mg * wells + w
        counts = jnp.where(here, cnt_ref[0, w].astype(F32), counts)
        bores = jnp.where(here, bhp_ref[0, w], bores)
    sw_send[1] = counts
    sw_send[2] = bores

    loads[0].wait()
    loads[1].wait()
    for z in range(zc):
        ysend_perm[0, z] = py[z * yc : z * yc + 1, :]
        ysend_perm[1, z] = py[z * yc + yc - 1 : z * yc + yc, :]

    pl.semaphore_wait(barrier, ng - 1 + nx - 1)
    perm_halos = halos(ysend_perm, yperm, pz, zperm, 0)
    for copy in perm_halos:
        copy.start()
    fan(group_peers, sw_send, sw_all.at[mg], 0)
    sw_all[mg] = sw_send[...]

    for d in range(ng):
        c = lane_spread(code, d, piece)
        rows = slice(d * 8, d * 8 + 8)
        hot_x[rows, :] = jnp.where(lane8 == jnp.bitwise_and(c, LANES - 1), 1.0, 0.0)
        for half in range(lines // LANES):
            hit = lane8 == jnp.right_shift(c, 7) - half * LANES
            line_sel[rows, half * LANES : half * LANES + LANES] = jnp.where(hit, 1.0, 0.0)
    line_sel_b[...] = line_sel[...].astype(BF16)
    line_sel_t[...] = line_sel[...].T.astype(BF16)

    loads[2].wait()
    loads[3].wait()
    lane_s = lane_of((yc, LANES))
    row_s = row_of((yc, LANES))
    for z in range(zc):
        rows = slice(z * yc, z * yc + yc)
        v = px[rows, :]
        f = jnp.where(lane_s == 0, 0.0, harmonic(pltpu.roll(v, 1, 1), v))
        left[rows, :] = f
        right[rows, :] = pltpu.roll(f, LANES - 1, 1)
        v = py[rows, :]
        f = harmonic(pltpu.roll(v, 1, 0), v)
        ylo[rows, :] = f
        if z > 0:
            zface[rows, :] = harmonic(pz[z * yc - yc : z * yc, :], pz[rows, :])
    strides = [1 << i for i in range(7)]

    def reduce_matrix(groups):
        for slices in groups:
            lo, hi, s = [jnp.concatenate([ref[rows, :] for rows in slices], axis=0) for ref in (left, right, sig)]
            lane_c = lane_of(lo.shape)

            def keep(ref, value, *at):
                start = 0
                for rows in slices:
                    size = rows.stop - rows.start
                    ref[(*at, rows, slice(None))] = value[start : start + size]
                    start += size

            for level, stride in enumerate(strides):
                r = 1.0 / (s + lo + hi)
                from_low = lane_c > stride
                from_high = lane_c < LANES - 1 - stride
                a = jnp.where(from_low, lo, 0.0)
                g = jnp.where(from_high, hi, 0.0)
                keep(low_m, a, level)
                keep(high_m, g, level)
                keep(recip, r, level)
                q = s * r
                s = s + a * pltpu.roll(q, stride, 1) + g * pltpu.roll(q, LANES - stride, 1)
                lo = jnp.where(from_low, lo * pltpu.roll(lo * r, stride, 1), lo)
                hi = jnp.where(from_high, hi * pltpu.roll(hi * r, LANES - stride, 1), hi)
            r = 1.0 / (s + lo + hi)
            first, last = lane_c == 0, lane_c == LANES - 1
            keep(inv, jnp.where(jnp.logical_or(first, last), 0.0, r))
            keep(low_w, jnp.where(first, 1.0, jnp.where(last, 0.0, lo * r)))
            keep(high_w, jnp.where(last, 1.0, jnp.where(first, 0.0, hi * r)))
            keep(sig, s)
            keep(right, hi)

    tile = 8
    inner = [[slice(z * yc + tile, z * yc + yc - tile) for z in range(1, zc - 1)]]
    edge = [slice(z * yc + o, z * yc + o + tile) for z in range(1, zc - 1) for o in (0, yc - tile)]
    cut = len(edge) // 2
    outer = [[slice(0, yc)] + edge[:cut], [slice(lines - yc, lines)] + edge[cut:]]
    for slices in inner:
        for rows in slices:
            sig[rows, :] = (
                st[rows, :] + ylo[rows, :] + ylo[rows.start + 1 : rows.stop + 1, :]
                + zface[rows, :] + zface[rows.start + yc : rows.stop + yc, :]
            )
    reduce_matrix(inner)

    for copy in perm_halos:
        copy.wait_recv()
    zface[0:yc, :] = jnp.where(mz == 0, 0.0, harmonic(zperm[0], pz[0:yc, :]))
    zface[lines : lines + yc, :] = jnp.where(mz == nz - 1, 0.0, harmonic(pz[lines - yc : lines, :], zperm[1]))
    for z in range(zc):
        rows = slice(z * yc, z * yc + yc)
        low = jnp.where(my == 0, 0.0, harmonic(yperm[0, z], py[z * yc : z * yc + 1, :]))
        top = jnp.where(my == ny - 1, 0.0, harmonic(py[z * yc + yc - 1 : z * yc + yc, :], yperm[1, z]))
        f = jnp.where(row_s == 0, low, ylo[rows, :])
        g = jnp.where(row_s == yc - 1, top, pltpu.roll(f, yc - 1, 0))
        ylo[rows, :] = f
        yup[rows, :] = g
        total = st[rows, :] + f + g + zface[rows, :] + zface[z * yc + yc : z * yc + 2 * yc, :]
        if z in (0, zc - 1):
            sig[rows, :] = total
        else:
            for o in (0, yc - tile):
                sig[z * yc + o : z * yc + o + tile, :] = total[o : o + tile]

    reduce_matrix(outer)

    def ends_of(ref):
        return pack_ends([ref[j * 8 : j * 8 + 8, :] for j in range(pieces)])

    stat_all[mx, 0] = ends_of(sig) + pltpu.roll(ends_of(px), LANES // 2, 1)
    stat_all[mx, 1] = ends_of(right)
    fan(x_peers, stat_all.at[mx], stat_all.at[mx], 1)

    def at_perforations(values):
        rows = onehot_product(line_sel_b[...], values)
        return jnp.sum(rows * hot_x[...], axis=1, keepdims=True)

    reach_first[...] = onehot_product(line_sel_t[...], hot_dw[...] * at_perforations(low_w[...]))
    reach_last[...] = onehot_product(line_sel_t[...], hot_dw[...] * at_perforations(high_w[...]))

    pair8 = lane8 // 2
    even = lane8 % 2 == 0

    def line_ends(for_first, for_last):
        packed = [jnp.zeros(piece, F32)] * 4
        for j in range(pieces):
            rows = slice(j * 8, j * 8 + 8)
            both = jnp.where(
                even,
                jnp.sum(for_last(rows), axis=1, keepdims=True),
                jnp.sum(for_first(rows), axis=1, keepdims=True),
            )
            packed[j % 4] = jnp.where(pair8 == j, both, packed[j % 4])
        return tree_sum(packed)

    def end_sources(values):
        return line_ends(lambda rows: low_w[rows, :] * values[rows, :], lambda rows: high_w[rows, :] * values[rows, :])

    def end_wells(seg_row):
        return line_ends(lambda rows: reach_first[rows, :] * seg_row, lambda rows: reach_last[rows, :] * seg_row)

    def send_ports(ports, packed, which):
        ports[mx] = packed + pltpu.roll(packed, LANES // 2, 1)
        fan(x_peers, ports.at[mx], ports.at[mx], which)

    def well_field(drop):
        back = jnp.sum(hot_dw[...] * drop, axis=1, keepdims=True)
        return onehot_product(line_sel_t[...], hot_x[...] * back)

    def solve_local():
        size = 128

        def part(i, carry):
            rows = pl.ds(pl.multiple_of(i * size, size), size)
            b = src[rows, :]
            for level, stride in enumerate(strides):
                t = b * recip[level, rows, :]
                b = b + low_m[level, rows, :] * pltpu.roll(t, stride, 1) + high_m[level, rows, :] * pltpu.roll(
                    t, LANES - stride, 1
                )
            src[rows, :] = b * inv[rows, :]
            return carry

        lax.fori_loop(0, lines // size, part, 0)

    def well_sums(cols):
        return jnp.sum(hot_dw[...] * cols, axis=0, keepdims=True)

    loads[4].wait()
    ends_rhs = end_sources(rhs)

    fan_wait(sw_all, ng - 1, fan_recv, 0)
    layer_all = [tree_sum(sw_all[y * nz + g] for y in range(ny)) for g in range(nz)]
    total = tree_sum(layer_all)
    count, bore = total[1], total[2]
    layer_sw = [layer[0] for layer in layer_all]

    def slot_of(g):
        return jnp.floor(g * count * (1.0 / nz))

    my_slot = slot_of(mz.astype(F32))
    layer_slots = [slot_of(float(g)) for g in range(nz)]
    same = [jnp.where(slot == my_slot, 1.0, 0.0) for slot in layer_slots]
    my_inv = 1.0 / (sum(m * sw for m, sw in zip(same, layer_sw)) + BORE)
    my_base = BORE * bore * my_inv
    send_ports(ports_a, ends_rhs + end_wells(my_base), 2)

    src[...] = rhs[...] + well_field(my_base)
    solve_local()
    row_own = well_sums(at_perforations(src[...]))

    fan_wait(stat_all, nx - 1, fan_recv, 1)

    def ends_at(k):
        s, c = stat_all[k, 0], stat_all[k, 1]
        return dict(
            sz=s, sf=pltpu.roll(s, LANES - 1, 1), pz=pltpu.roll(s, LANES // 2, 1),
            pf=pltpu.roll(s, LANES // 2 - 1, 1), c=pltpu.roll(c, LANES - 1, 1),
        )

    own = ends_at(mx)

    def walk(direction):
        chain = []
        for t in range(1, nx):
            k = mx + direction * t
            valid = jnp.logical_and(k >= 0, k < nx)
            chain.append((jnp.clip(k, 0, nx - 1), valid))
        blocks = [ends_at(k) for k, _ in chain]
        ground = jnp.zeros(piece, F32)
        factors = [None] * (nx - 1)
        for t in range(nx - 1, 0, -1):
            b = blocks[t - 1]
            nearer = own if t == 1 else blocks[t - 2]
            far, near, edge = ("sf", "sz", ("pz", "pf")) if direction < 0 else ("sz", "sf", ("pf", "pz"))
            face = jnp.where(chain[t - 1][1], harmonic(b[edge[0]], nearer[edge[1]]), 0.0)
            shunt = b[far] + ground
            joined = b["c"] + shunt
            inner = b[near] * joined + shunt * b["c"]
            part = face / (face * joined + inner)
            ground = inner * part
            factors[t - 1] = (part * joined, part * b["c"])
        reach = jnp.ones(piece, F32)
        weights = []
        for from_near, from_far in factors:
            weights.append((reach * from_near, reach * from_far))
            reach = weights[-1][1]
        return ground, weights, [k for k, _ in chain]

    ground_l, weights_l, index_l = walk(-1)
    ground_r, weights_r, index_r = walk(1)
    a, e, c = own["sf"] + ground_l, own["sz"] + ground_r, own["c"]
    scale = 1.0 / (a * e + (a + e) * c)
    ff, fz, zz = (e + c) * scale, c * scale, (a + c) * scale
    lower_half = lane8 < LANES // 2

    def weave(z_first, f_first, z_last, f_last):
        first = jnp.where(even, z_first, pltpu.roll(f_first, 1, 1))
        last = jnp.where(even, pltpu.roll(z_last, LANES // 2, 1), pltpu.roll(f_last, LANES // 2 + 1, 1))
        return jnp.where(lower_half, first, last)

    terms = [(mx, weave(fz, ff, zz, fz))]
    for (near_w, far_w), k in zip(weights_l, index_l):
        terms.append((k, weave(ff * near_w, ff * far_w, fz * near_w, fz * far_w)))
    for (near_w, far_w), k in zip(weights_r, index_r):
        terms.append((k, weave(fz * far_w, fz * near_w, zz * far_w, zz * near_w)))

    def end_pressures(ports):
        ends = tree_sum(w * ports[k] for k, w in terms)
        ends = ends + pltpu.roll(ends, LANES - 1, 1)
        return [
            (lane_spread(ends, 2 * j, piece), lane_spread(ends, LANES // 2 + 2 * j, piece)) for j in range(pieces)
        ]

    def end_sums(ends):
        lanes = [0.0] * 8
        for j, (first, last) in enumerate(ends):
            rows = slice(j * 8, j * 8 + 8)
            lanes[j % 8] = lanes[j % 8] + (reach_first[rows, :] * first + reach_last[rows, :] * last)
        return jnp.sum(tree_sum(lanes), axis=0, keepdims=True)

    def join(ends, target):
        for j, (first, last) in enumerate(ends):
            rows = slice(j * 8, j * 8 + 8)
            target[rows, :] = src[rows, :] + low_w[rows, :] * first + high_w[rows, :] * last

    def send_row(which, row, target):
        row_send[which] = row
        fan(group_peers, row_send.at[which], target.at[mg], 3 + which)
        target[mg] = row

    fan_wait(ports_a, nx - 1, fan_recv, 2)
    ends = end_pressures(ports_a)
    send_row(0, row_own + end_sums(ends), rows_a)

    join(ends, field)
    for z in range(zc):
        ysend_p[0, z] = field[z * yc : z * yc + 1, :]
        ysend_p[1, z] = field[z * yc + yc - 1 : z * yc + yc, :]
    p_halos = halos(ysend_p, yp, field, zp, 4)
    for copy in p_halos:
        copy.start()
    cols = at_perforations(field[...])
    coef_mine = [m * my_inv for m in same]
    coef_seg = []
    for g in range(nz):
        slot_sw = sum(jnp.where(layer_slots[h] == layer_slots[g], layer_sw[h], 0.0) for h in range(nz))
        coef_seg.append(1.0 / (slot_sw + BORE))
    residual_base = bore * sum(f * sw for f, sw in zip(coef_seg, layer_sw))

    for copy in p_halos:
        copy.wait_recv()
    for z in range(zc):
        rows = slice(z * yc, z * yc + yc)
        v = field[rows, :]
        below = jnp.where(row_s == 0, yp[0, z], pltpu.roll(v, 1, 0))
        above = jnp.where(row_s == yc - 1, yp[1, z], pltpu.roll(v, yc - 1, 0))
        under = field[z * yc - yc : z * yc, :] if z > 0 else zp[0]
        over = field[z * yc + yc : z * yc + 2 * yc, :] if z < zc - 1 else zp[1]
        beside = ylo[rows, :] * below + yup[rows, :] * above
        beside = beside + zface[rows, :] * under + zface[z * yc + yc : z * yc + 2 * yc, :] * over
        src[rows, :] = rhs[rows, :] + beside
    src[...] = src[...] + well_field(my_base - cols)
    ends_base = end_sources(src)

    fan_wait(rows_a, ng - 1, fan_recv, 3)
    inflow = tree_sum(f * tree_sum(rows_a[y * nz + g] for y in range(ny)) for g, f in enumerate(coef_mine))
    send_ports(ports_b, ends_base + end_wells(inflow), 5)
    src[...] = src[...] + well_field(inflow)
    solve_local()
    row_own = well_sums(at_perforations(src[...]))
    fan_wait(ports_b, nx - 1, fan_recv, 5)
    ends = end_pressures(ports_b)
    send_row(1, row_own + end_sums(ends), rows_b)
    join(ends, p_out)
    fan_wait(rows_b, ng - 1, fan_recv, 4)
    res = tree_sum(f * tree_sum(rows_b[y * nz + g] for y in range(ny)) for g, f in enumerate(coef_seg)) - residual_base
    res_out[...] = pltpu.roll(res, lax.rem(LANES - mg * wells, LANES), 1)[:, :wells]

    for copy in perm_halos + p_halos:
        copy.wait_send()
    fan_wait(sw_all, ng - 1, fan_send, 0)
    fan_wait(stat_all, nx - 1, fan_send, 1)
    fan_wait(ports_a, nx - 1, fan_send, 2)
    fan_wait(rows_a, ng - 1, fan_send, 3)
    fan_wait(rows_b, ng - 1, fan_send, 4)
    fan_wait(ports_b, nx - 1, fan_send, 5)


def shards(dims, rhs, perm_x, perm_y, perm_z, storage, perf_cell, perf_well, perf_index, seg_count, bhp):
    nx, ny, nz, zc, yc, wells = dims
    ng = ny * nz
    lines = zc * yc
    perfs = ng * 8
    plane = (lines, LANES)
    flat = [a.reshape(plane) for a in (rhs, perm_x, perm_y, perm_z, storage)]
    slots = [a[0, 0].T for a in (perf_cell, perf_well, perf_index)]
    operands = [pltpu.with_memory_space_constraint(a, pltpu.HBM) for a in (*slots, seg_count[0], bhp[0], *flat)]
    vmem = pl.BlockSpec(memory_space=pltpu.VMEM)
    hbm = pl.BlockSpec(memory_space=pltpu.HBM)
    whole = pltpu.VMEM(plane, F32)
    perf_plane = pltpu.VMEM((perfs, LANES), F32)
    pressure, residual = pl.pallas_call(
        functools.partial(kernel, dims),
        out_shape=(pltpu.VMEM(plane, F32), pltpu.VMEM((1, wells), F32)),
        in_specs=[hbm] * 10,
        out_specs=(vmem, vmem),
        scratch_shapes=[pltpu.VMEM((8, ng), jnp.int32)] * 2
        + [pltpu.VMEM((8, ng), F32), pltpu.SMEM((1, wells), jnp.int32), pltpu.SMEM((1, wells), F32)]
        + [whole] * 5
        + [whole] * 5
        + [pltpu.VMEM((lines + yc, LANES), F32)]
        + [pltpu.VMEM((7, lines, LANES), F32)] * 3
        + [whole] * 5
        + [perf_plane] * 2
        + [pltpu.VMEM((perfs, lines), F32), pltpu.VMEM((perfs, lines), BF16), pltpu.VMEM((lines, perfs), BF16)]
        + [whole] * 2
        + [pltpu.VMEM((2, zc, 1, LANES), F32), pltpu.VMEM((2, yc, LANES), F32)]
        + [pltpu.VMEM((2, zc, 1, LANES), F32)] * 3
        + [pltpu.VMEM((2, yc, LANES), F32)]
        + [pltpu.VMEM((3, 1, LANES), F32), pltpu.VMEM((ng, 3, 1, LANES), F32)]
        + [pltpu.VMEM((2, 1, LANES), F32)]
        + [pltpu.VMEM((ng, 1, LANES), F32)] * 2
        + [pltpu.VMEM((nx, 2, 8, LANES), F32)]
        + [pltpu.VMEM((nx, 8, LANES), F32)] * 2
        + [
            pltpu.SemaphoreType.DMA((10,)),
            pltpu.SemaphoreType.DMA((8,)),
            pltpu.SemaphoreType.DMA((8,)),
            pltpu.SemaphoreType.DMA((6,)),
            pltpu.SemaphoreType.DMA((6,)),
        ],
        compiler_params=pltpu.CompilerParams(
            collective_id=0, has_side_effects=True, vmem_limit_bytes=32 * 1024 * 1024
        ),
        name="sweeps",
    )(*operands)
    return pressure.reshape(rhs.shape), residual.reshape(1, 1, wells)


def solution(mesh):
    nx, ny, nz = mesh.shape["gx"], mesh.shape["gy"], mesh.shape["gz"]
    cells = P("gz", "gy", "gx")
    perfs = P("gx", ("gy", "gz"), None, None)
    owned = P("gx", ("gy", "gz"), None)

    def program(rhs, perm_x, perm_y, perm_z, storage, perf_cell, perf_well, perf_index, seg_count, bhp):
        dims = (nx, ny, nz, rhs.shape[0] // nz, rhs.shape[1] // ny, seg_count.shape[-1])
        return jax.shard_map(
            functools.partial(shards, dims),
            mesh=mesh,
            in_specs=(cells,) * 5 + (perfs,) * 3 + (owned,) * 2,
            out_specs=(cells, owned),
            check_vma=False,
        )(rhs, perm_x, perm_y, perm_z, storage, perf_cell, perf_well, perf_index, seg_count, bhp)

    return program
```
